32 devices in a mesh: groups: 2 (over x), seq: 8 (over z, y), chan: 2 (over core).
Axes of the slice: x: 2, y: 2, z: 4, core: 2. Of those that a mesh axis runs over, the one named last changes fastest.
Arguments:
- tower_input: bfloat16 [16384, 1536], P(('groups', 'seq'), 'chan'), parts along dimension 0, may hold values from -6 to 6
- dna_bases: int32 [16384, 32], P(('groups', 'seq')), parts along dimension 0, may hold values from 0 to 3
- base_embed: bfloat16 [128, 1536], P(None, 'chan'), may hold values from -1 to 1
- in_scale: float32 [2, 1536], P(None, 'chan'), may hold values from 0.5 to 1.5
- entry_norm_shift: float32 [2, 1536], P(None, 'chan'), may hold values from -0.5 to 0.5
- conv_w: bfloat16 [2, 3, 1536, 768], P(None, None, 'chan'), may hold values from -0.09375 to 0.09375
- mid_scale: float32 [2, 768], P(None, 'chan'), may hold values from 0.5 to 1.5
- mid_shift: float32 [2, 768], P(None, 'chan'), may hold values from -0.5 to 0.5
- point_w: bfloat16 [2, 768, 1536], P(None, None, 'chan'), may hold values from -0.21875 to 0.21875
- pooling_weight: bfloat16 [1536, 1536], P(None, 'chan'), may hold values from -0.15625 to 0.15625
Outputs:
- pooled: bfloat16 [8192, 1536], P(('groups', 'seq'), 'chan'), parts along dimension 0
The draws below stay inside these ranges and needn't reach their ends.
There are 2 independent parts, one for each index of `groups`. The reference program is written for one: setup_inputs(seed, part) draws one part's arguments, and reference() takes and returns one part's arrays. A program takes and returns all parts, laid end to end along the dimension named above; an argument that names none is the same for every part. Nothing has to cross between parts.
All inputs are finite; a program needn't handle non-finite values.
Results may differ from the reference program's by a relative error of at most 0.018.
Values may be sent and summed in bfloat16 or wider, within the bound.
No kernel may reach another device: no remote copies, remote signals or barrier semaphores. Data moves between devices by JAX's collectives and lax.ppermute only.
A program may use at most 128 MiB of HBM per device.

```python
import jax
import jax.numpy as jnp

C = 1536
B = 768
BASES = 32
NBLK = 2
FIRST_SPACING = 32
SECOND_SPACING = 48
BINS = 8192


def touch_ends(values, own_key, low, top_value):
    index_at = [jax.random.randint(jax.random.fold_in(own_key, axis), (), 0, length) for axis, length in enumerate(values.shape)]
    main_axis = values.shape.index(max(values.shape))
    neighbour = index_at[:main_axis] + [(index_at[main_axis] + 1) % values.shape[main_axis]] + index_at[main_axis + 1:]
    return values.at[tuple(index_at)].set(low).at[tuple(neighbour)].set(top_value)


def shard_levels(rng, extent, cuts, least, top_value):
    factor_of = 1.0
    for dim, blocks in cuts:
        draws = jax.random.uniform(jax.random.fold_in(jax.random.fold_in(rng, 6), dim), (blocks,), jnp.float32, least / len(cuts), top_value / len(cuts))
        factor_of = factor_of * jnp.repeat(jnp.exp(draws), extent[dim] // blocks).reshape((-1,) + (1,) * (len(extent) - 1 - dim))
    return factor_of


def scatter_about(key, shape, deviation, limit, shards=(), held_as=jnp.bfloat16):
    entries = deviation * jax.random.normal(key, shape, jnp.float32)
    if shards:
        entries = entries * shard_levels(key, shape, shards, -0.22, 0.18)
    return jnp.clip(entries, -limit, limit).astype(held_as)


def setup_inputs(seed: int = 0, part: int = 0) -> dict:
    keys = jax.random.split(jax.random.key(seed), 11)
    part_keys = jax.random.split(jax.random.fold_in(keys[10], part), 11)
    tower_input = scatter_about(part_keys[0], (BINS, C), 1.0, 6.0, ((0, 8), (1, 2)))
    dna_bases = touch_ends(jax.random.randint(part_keys[1], (BINS, BASES), 0, 4), jax.random.fold_in(part_keys[1], 1), 0, 3).astype(jnp.int32)
    base_embed = scatter_about(keys[2], (4 * BASES, C), BASES ** -0.5, 1.0, ((1, 2),))
    in_scale = jnp.clip(1.0 + 0.1 * jax.random.normal(keys[3], (NBLK, C), jnp.float32), 0.5, 1.5)
    entry_norm_shift = jnp.clip(jax.random.uniform(keys[4], (NBLK, C), jnp.float32, -0.5, 0.5) * shard_levels(keys[4], (NBLK, C), ((1, 2),), -0.4, 0.0), -0.5, 0.5)
    conv_w = scatter_about(keys[5], (NBLK, 3, C, B), (3 * C) ** -0.5, 0.09375, ((2, 2),))
    mid_scale = jnp.clip(1.0 + 0.1 * jax.random.normal(keys[6], (NBLK, B), jnp.float32), 0.5, 1.5)
    mid_shift = jnp.clip(jax.random.uniform(keys[7], (NBLK, B), jnp.float32, -0.5, 0.5) * shard_levels(keys[7], (NBLK, B), ((1, 2),), -0.4, 0.0), -0.5, 0.5)
    point_w = scatter_about(keys[8], (NBLK, B, C), B ** -0.5, 0.21875, ((2, 2),))
    pooling_weight = scatter_about(keys[9], (C, C), C ** -0.5, 0.15625, ((1, 2),))
    return dict(tower_input=tower_input, dna_bases=dna_bases, base_embed=base_embed, in_scale=in_scale, entry_norm_shift=entry_norm_shift, conv_w=conv_w, mid_scale=mid_scale, mid_shift=mid_shift, point_w=point_w, pooling_weight=pooling_weight)


def gelu_tanh(value):
    return jax.nn.gelu(value, approximate=True)


def reference(tower_input, dna_bases, base_embed, in_scale, entry_norm_shift, conv_w, mid_scale, mid_shift, point_w, pooling_weight):
    length = tower_input.shape[0]
    onehot = (dna_bases[:, :, None] == jnp.arange(4, dtype=jnp.int32)[None, None, :]).astype(jnp.bfloat16)
    onehot = onehot.reshape(length, 4 * BASES)
    stream = (tower_input.astype(jnp.float32) + jnp.dot(onehot, base_embed, preferred_element_type=jnp.float32)).astype(jnp.bfloat16)
    spacing_list = (FIRST_SPACING, SECOND_SPACING)
    for layer_idx in range(NBLK):
        spread = spacing_list[layer_idx]
        act = gelu_tanh(stream.astype(jnp.float32) * in_scale[layer_idx] + entry_norm_shift[layer_idx]).astype(jnp.bfloat16)
        padded = jnp.pad(act, ((spread, spread), (0, 0)))
        partial_value = jnp.dot(padded[0:length], conv_w[layer_idx, 0], preferred_element_type=jnp.float32)
        partial_value = partial_value + jnp.dot(act, conv_w[layer_idx, 1], preferred_element_type=jnp.float32)
        partial_value = partial_value + jnp.dot(padded[2 * spread:2 * spread + length], conv_w[layer_idx, 2], preferred_element_type=jnp.float32)
        inner = gelu_tanh(partial_value * mid_scale[layer_idx] + mid_shift[layer_idx]).astype(jnp.bfloat16)
        update = jnp.dot(inner, point_w[layer_idx], preferred_element_type=jnp.float32)
        stream = (stream.astype(jnp.float32) + update).astype(jnp.bfloat16)
    score_logits = jnp.dot(stream, pooling_weight, preferred_element_type=jnp.float32)
    width = stream.shape[1]
    pairs = stream.astype(jnp.float32).reshape(length // 2, 2, width)
    logit_pairs = score_logits.reshape(length // 2, 2, width)
    weight_first = jax.nn.sigmoid(logit_pairs[:, 0] - logit_pairs[:, 1])
    result = pairs[:, 1] + weight_first * (pairs[:, 0] - pairs[:, 1])
    return result.astype(jnp.bfloat16)
```

```python
import jax
import jax.numpy as jnp
from jax import lax
from jax.experimental import pallas as pl
from jax.experimental.pallas import tpu as pltpu
from jax.sharding import PartitionSpec as P

D0 = 32
D1 = 48
HALO = D0 + D1
EXTRA = 16
BF = jnp.bfloat16
F32 = jnp.float32
VM = pl.BlockSpec(memory_space=pltpu.VMEM)
HBM = pl.BlockSpec(memory_space=pltpu.HBM)
GRANT = 14 << 20


def call(kernel, outs, hbm, vmem, scratch=(), grant=GRANT):
    hbm = [pltpu.with_memory_space_constraint(a, pltpu.HBM) for a in hbm]
    vmem = [pltpu.with_memory_space_constraint(a, pltpu.VMEM) for a in vmem]
    return pl.pallas_call(
        kernel,
        out_shape=[pltpu.VMEM(shape, dtype) for shape, dtype in outs],
        in_specs=[HBM] * len(hbm) + [VM] * len(vmem),
        out_specs=[VM] * len(outs),
        scratch_shapes=list(scratch),
        compiler_params=pltpu.CompilerParams(vmem_limit_bytes=grant),
    )(*hbm, *vmem)


def gelu(v):
    inner = v * (0.7978845608028654 + 0.035677408136300125 * (v * v))
    half = 0.5 * v
    return half + half * jnp.tanh(inner)


def dot(a, b):
    return jnp.dot(a, b, preferred_element_type=F32)


def tiles(start, stop, step):
    return [(i, min(step, stop - i)) for i in range(start, stop, step)]


def act_rows(x, s_ref, b_ref, layer):
    return gelu(x.astype(F32) * s_ref[layer : layer + 1] + b_ref[layer : layer + 1]).astype(BF)


def conv_rows(h_ref, base, spread, n, w_ref):
    lhs = jnp.concatenate(
        [h_ref[base + k * spread : base + k * spread + n] for k in (-1, 0, 1)], axis=1
    )
    return dot(lhs, w_ref[...])


def mid_rows(own, other, mid_ref, layer):
    u = own.astype(F32) + other.astype(F32)
    return gelu(u * mid_ref[layer : layer + 1] + mid_ref[2 + layer : 3 + layer]).astype(BF)


def embed_first(a_lo, a_hi, rows, width):
    def kernel(
        tower, dna, embed, ins, inb, conv_w, mids, midb, point_w,
        x0, h0, e_a, e_b, pa, w0, pw0, w1, s_in, b_in, own_mid,
        tower_v, dna_v, embed_v, mids_v, midb_v, sem,
    ):
        cp = pltpu.make_async_copy
        half = rows // 2
        c_dna = cp(dna, dna_v, sem.at[0])
        c_emb = cp(embed, embed_v, sem.at[1])
        c_tow = [
            cp(tower.at[pl.ds(i * half, half)], tower_v.at[pl.ds(i * half, half)], sem.at[2 + i])
            for i in range(2)
        ]
        c_s = cp(ins, s_in, sem.at[4])
        c_b = cp(inb, b_in, sem.at[5])
        c_ms = cp(mids, mids_v, sem.at[6])
        c_mb = cp(midb, midb_v, sem.at[7])
        c_w0 = [
            cp(conv_w.at[0, k], w0.at[pl.ds(k * width, width)], sem.at[8 + k]) for k in range(3)
        ]
        c_pw = cp(point_w.at[0], pw0, sem.at[11])
        c_w1 = [
            cp(conv_w.at[1, k], w1.at[pl.ds(k * width, width)], sem.at[12 + k]) for k in range(3)
        ]
        for c in [c_dna, c_emb, *c_tow, c_s, c_b, c_ms, c_mb, *c_w0, c_pw, *c_w1]:
            c.start()
        slots = dna.shape[0]
        row = lax.broadcasted_iota(jnp.int32, (4 * slots, slots), 0)
        col = lax.broadcasted_iota(jnp.int32, (4 * slots, slots), 1)
        spread_map = jnp.where((row >> 2) == col, 1.0, 0.0).astype(BF)
        c_dna.wait()
        c_emb.wait()
        c_s.wait()
        c_b.wait()
        for i, n in tiles(0, rows, 128):
            if i % half == 0:
                c_tow[i // half].wait()
            code = (lax.broadcasted_iota(jnp.int32, (4 * slots, n), 0) & 3).astype(F32)
            base = dot(spread_map, dna_v[:, i : i + n].astype(F32).astype(BF))
            onehot = jnp.where(base == code, 1.0, 0.0).T.astype(BF)
            x = (tower_v[i : i + n].astype(F32) + dot(onehot, embed_v[...])).astype(BF)
            x0[i : i + n] = x
            h0[i : i + n] = act_rows(x, s_in, b_in, 0)
        even = lax.rem(lax.axis_index("seq"), 2) == 0
        low = x0[0:HALO]
        high = x0[rows - HALO : rows]
        e_a[...] = jnp.where(even, high, low)
        e_b[...] = jnp.where(even, low, high)
        c_ms.wait()
        c_mb.wait()
        first = lax.axis_index("chan") == 0
        mid = jnp.concatenate([mids_v[...], midb_v[...]], axis=0)
        mid = jnp.concatenate(
            [jnp.where(first, mid, 0.0), jnp.where(first, 0.0, mid)], axis=1
        )
        own_mid[...] = mid
        big = mid.astype(BF)
        rest = mid - big.astype(F32)
        middle = rest.astype(BF)
        small = (rest - middle.astype(F32)).astype(BF)
        pa[a_hi - a_lo : a_hi - a_lo + EXTRA] = jnp.concatenate(
            [big.astype(F32), middle.astype(F32), small.astype(F32), jnp.zeros_like(mid)], axis=0
        ).astype(BF)
        for c in c_w0:
            c.wait()
        for i, n in tiles(a_lo, a_hi, 256):
            pa[i - a_lo : i - a_lo + n] = conv_rows(h0, i, D0, n, w0).astype(BF)
        c_pw.wait()
        for c in c_w1:
            c.wait()

    return kernel


def first_rest(b_lo, b_hi):
    def kernel(point_w, pool_w, h0, w0, pb, pw1, pool, sem):
        copies = [
            pltpu.make_async_copy(point_w.at[1], pw1, sem.at[0]),
            pltpu.make_async_copy(pool_w, pool, sem.at[1]),
        ]
        for c in copies:
            c.start()
        for i, n in tiles(b_lo, b_hi, 224):
            pb[i - b_lo : i - b_lo + n] = conv_rows(h0, i, D0, n, w0).astype(BF)
        for c in copies:
            c.wait()

    return kernel


def first_edges(rows):
    def kernel(r_a, r_b, h0, w0, s_in, b_in, pe, lo, hi, ext):
        seq = lax.axis_index("seq")
        even = lax.rem(seq, 2) == 0
        low = jnp.where(even, r_b[...], r_a[...])
        high = jnp.where(even, r_a[...], r_b[...])
        lo[...] = low
        hi[...] = high
        zero = jnp.zeros(low.shape, BF)
        inner = 2 * D0
        span = HALO + inner
        ext[0:HALO] = jnp.where(seq == 0, zero, act_rows(low, s_in, b_in, 0))
        ext[HALO:span] = h0[0:inner]
        ext[span : span + inner] = h0[rows - inner : rows]
        ext[span + inner : 2 * span] = jnp.where(
            seq == lax.axis_size("seq") - 1, zero, act_rows(high, s_in, b_in, 0)
        )
        lhs = [
            jnp.concatenate(
                [ext[s + k * D0 : s + k * D0 + HALO] for k in range(3)], axis=1
            )
            for s in (0, span)
        ]
        pe[...] = dot(jnp.concatenate(lhs, axis=0), w0[...]).astype(BF)

    return kernel


def second_first(a_lo, a_hi, c_lo, c_hi):
    def kernel(pa, ra, x0, pw0, w1, s_in, b_in, own_mid, x1a, h1a, qa, mid):
        n_a = a_hi - a_lo
        tail = ra[n_a : n_a + EXTRA].astype(F32)
        mid[...] = own_mid[...] + (tail[0:4] + tail[4:8] + tail[8:12])
        for i, n in tiles(0, n_a, 256):
            z = mid_rows(pa[i : i + n], ra[i : i + n], mid, 0)
            x = (x0[a_lo + i : a_lo + i + n].astype(F32) + dot(z, pw0[...])).astype(BF)
            x1a[i : i + n] = x
            h1a[i : i + n] = act_rows(x, s_in, b_in, 1)
        for i, n in tiles(c_lo, c_hi, 192):
            qa[i - c_lo : i - c_lo + n] = conv_rows(h1a, i - a_lo, D1, n, w1).astype(BF)

    return kernel


def second_rest(rows, a_lo, a_hi, c_lo, c_hi):
    def kernel(
        pb, rb, pe, re, x0, lo, hi, x1a, h1a, pw0, w1, mid, s_in, b_in, x1b, qb, h1
    ):
        seq = lax.axis_index("seq")
        b_hi = rows - D0
        for i, n in tiles(0, b_hi - a_hi, 224):
            z = mid_rows(pb[i : i + n], rb[i : i + n], mid, 0)
            g = a_hi + i
            x = (x0[g : g + n].astype(F32) + dot(z, pw0[...])).astype(BF)
            x1b[c_lo + g - c_hi : c_lo + g - c_hi + n] = x
            h1[D1 + g : D1 + g + n] = act_rows(x, s_in, b_in, 1)
        z = mid_rows(pe[...], re[...], mid, 0)
        base = jnp.concatenate(
            [lo[HALO - D1 : HALO], x0[0:D0], x0[rows - D0 : rows], hi[0:D1]], axis=0
        )
        x = (base.astype(F32) + dot(z, pw0[...])).astype(BF)
        x1b[0:D0] = x[D1 : D1 + D0]
        x1b[D0:c_lo] = x1a[0 : c_lo - a_lo]
        x1b[c_lo : c_lo + a_hi - c_hi] = x1a[c_hi - a_lo : a_hi - a_lo]
        x1b[c_lo + b_hi - c_hi : c_lo + rows - c_hi] = x[HALO : HALO + D0]
        h = act_rows(x, s_in, b_in, 1)
        zero = jnp.zeros((D1, h.shape[1]), BF)
        h1[0:D1] = jnp.where(seq == 0, zero, h[0:D1])
        h1[D1:HALO] = h[D1:HALO]
        h1[D1 + b_hi : D1 + rows] = h[HALO : HALO + D0]
        h1[D1 + rows : 2 * D1 + rows] = jnp.where(
            seq == lax.axis_size("seq") - 1, zero, h[HALO + D0 :]
        )
        keep = 2 * D1
        h1[D1 + a_lo : D1 + c_lo + D1] = h1a[0 : c_lo + D1 - a_lo]
        h1[D1 + c_hi - D1 : D1 + a_hi] = h1a[c_hi - D1 - a_lo : a_hi - a_lo]
        qb[0:c_lo] = conv_rows(h1, D1, D1, c_lo, w1).astype(BF)
        for i, n in tiles(c_hi, rows, 272):
            qb[c_lo + i - c_hi : c_lo + i - c_hi + n] = conv_rows(h1, D1 + i, D1, n, w1).astype(BF)

    return kernel


def last_point(x_base, n_rows, step):
    def kernel(q, r, x1, pw1, mid, dm, df, xo, wide):
        for i, n in tiles(0, n_rows, step):
            z = mid_rows(q[i : i + n], r[i : i + n], mid, 1)
            x = x1[x_base + i : x_base + i + n].astype(F32) + dot(z, pw1[...])
            x = x.astype(BF).astype(F32)
            j, m = i // 2, n // 2
            for k in range(wide.shape[0]):
                cols = slice(128 * k, 128 * (k + 1))
                wide[k, i : i + n] = x[:, cols]
                first = wide[k, pl.ds(i, m, stride=2), :]
                second = wide[k, pl.ds(i + 1, m, stride=2), :]
                d = first - second
                dm[j : j + m, cols] = d.astype(BF)
                df[j : j + m, cols] = d
                xo[j : j + m, cols] = second.astype(BF)

    return kernel


def pool_first(da, ra, db, pool, dfa, xoa, ya, lb):
    width = da.shape[1]
    chan = lax.axis_index("chan")
    mine = pl.ds(pl.multiple_of(chan * width, 128), width)
    theirs = pl.ds(pl.multiple_of((1 - chan) * width, 128), width)
    lb[...] = dot(db[...], pool[mine, :])
    logit = dot(da[...], pool[mine, :]) + dot(ra[...], pool[theirs, :])
    ya[...] = (xoa[...].astype(F32) + jax.nn.sigmoid(logit) * dfa[...]).astype(BF)


def pool_last(p_lo, p_hi, pairs):
    def kernel(rb, lb, pool, dfb, xob, ya, out, y, sem):
        width = rb.shape[1]
        chan = lax.axis_index("chan")
        theirs = pl.ds(pl.multiple_of((1 - chan) * width, 128), width)
        copies = [pltpu.make_async_copy(ya, out.at[pl.ds(p_lo, p_hi - p_lo)], sem.at[0])]
        copies[0].start()
        for slot, (i, n) in enumerate([(0, p_lo)] + tiles(p_lo, rb.shape[0], 160)):
            logit = lb[i : i + n] + dot(rb[i : i + n], pool[theirs, :])
            y[i : i + n] = (
                xob[i : i + n].astype(F32) + jax.nn.sigmoid(logit) * dfb[i : i + n]
            ).astype(BF)
            at = i if i < p_lo else i - p_lo + p_hi
            copies.append(
                pltpu.make_async_copy(
                    y.at[pl.ds(i, n)], out.at[pl.ds(at, n)], sem.at[1 + slot]
                )
            )
            copies[-1].start()
        for c in copies:
            c.wait()

    return kernel


def swap_chan(a):
    return lax.ppermute(a, "chan", [(0, 1), (1, 0)])


def local(
    tower_input, dna_bases, base_embed, in_scale, entry_norm_shift,
    conv_w, mid_scale, mid_shift, point_w, pooling_weight,
):
    rows, width = tower_input.shape
    inner = conv_w.shape[3]
    a_lo, a_hi = D0, rows // 2 + 32
    c_lo, c_hi = 96, rows // 2 - 32
    b_hi = rows - D0
    n_a, n_b = a_hi - a_lo, b_hi - a_hi
    m_a = c_hi - c_lo
    m_b = rows - m_a
    dma = pltpu.SemaphoreType.DMA
    x0, h0, e_a, e_b, pa, w0, pw0, w1, s_in, b_in, own_mid = call(
        embed_first(a_lo, a_hi, rows, width),
        [
            ((rows, width), BF), ((rows, width), BF), ((HALO, width), BF), ((HALO, width), BF),
            ((n_a + EXTRA, inner), BF), ((3 * width, inner), BF), ((inner, width), BF),
            ((3 * width, inner), BF), ((2, width), F32), ((2, width), F32), ((4, inner), F32),
        ],
        [
            tower_input, dna_bases.T, base_embed, in_scale, entry_norm_shift, conv_w,
            mid_scale, mid_shift, point_w,
        ],
        [],
        [
            pltpu.VMEM((rows, width), BF), pltpu.VMEM(dna_bases.shape[::-1], jnp.int32),
            pltpu.VMEM(base_embed.shape, BF), pltpu.VMEM(mid_scale.shape, F32),
            pltpu.VMEM(mid_shift.shape, F32), dma((15,)),
        ],
    )
    ra = swap_chan(pa)
    count = lax.axis_size("seq")
    pairs_a = [(i, i ^ 1) for i in range(count)]
    pairs_b = [(i, ((i - 1) ^ 1) + 1) for i in range(1, count - 1)]
    r_a = lax.ppermute(e_a, "seq", pairs_a)
    r_b = lax.ppermute(e_b, "seq", pairs_b)
    pb, pw1, pool = call(
        first_rest(a_hi, b_hi),
        [((n_b, inner), BF), ((inner, width), BF), (pooling_weight.shape, BF)],
        [point_w, pooling_weight],
        [h0, w0],
        [dma((2,))],
    )
    rb = swap_chan(pb)
    pe, lo, hi = call(
        first_edges(rows),
        [((2 * HALO, inner), BF), ((HALO, width), BF), ((HALO, width), BF)],
        [],
        [r_a, r_b, h0, w0, s_in, b_in],
        [pltpu.VMEM((2 * (HALO + 2 * D0), width), BF)],
    )
    re = swap_chan(pe)
    x1a, h1a, qa, mid = call(
        second_first(a_lo, a_hi, c_lo, c_hi),
        [((n_a, width), BF), ((n_a, width), BF), ((m_a, inner), BF), ((4, inner), F32)],
        [],
        [pa, ra, x0, pw0, w1, s_in, b_in, own_mid],
    )
    sa = swap_chan(qa)
    x1b, qb = call(
        second_rest(rows, a_lo, a_hi, c_lo, c_hi),
        [((m_b, width), BF), ((m_b, inner), BF)],
        [],
        [pb, rb, pe, re, x0, lo, hi, x1a, h1a, pw0, w1, mid, s_in, b_in],
        [pltpu.VMEM((rows + 2 * D1, width), BF)],
    )
    sb = swap_chan(qb)
    da, dfa, xoa = call(
        last_point(c_lo - a_lo, m_a, 192),
        [((m_a // 2, width), BF), ((m_a // 2, width), F32), ((m_a // 2, width), BF)],
        [],
        [qa, sa, x1a, pw1, mid],
        [pltpu.VMEM((width // 128, m_a, 128), F32)],
    )
    ta = swap_chan(da)
    db, dfb, xob = call(
        last_point(0, m_b, 160),
        [((m_b // 2, width), BF), ((m_b // 2, width), F32), ((m_b // 2, width), BF)],
        [],
        [qb, sb, x1b, pw1, mid],
        [pltpu.VMEM((width // 128, m_b, 128), F32)],
    )
    tb = swap_chan(db)
    ya, lb = call(
        pool_first,
        [((m_a // 2, width), BF), ((m_b // 2, width), F32)],
        [],
        [da, ta, db, pool, dfa, xoa],
    )
    vm = [pltpu.with_memory_space_constraint(a, pltpu.VMEM) for a in (tb, lb, pool, dfb, xob, ya)]
    return pl.pallas_call(
        pool_last(c_lo // 2, c_hi // 2, rows // 2),
        out_shape=jax.ShapeDtypeStruct((rows // 2, width), BF),
        in_specs=[VM] * 6,
        out_specs=HBM,
        scratch_shapes=[pltpu.VMEM((m_b // 2, width), BF), dma((8,))],
        compiler_params=pltpu.CompilerParams(vmem_limit_bytes=GRANT),
    )(*vm)


def solution(mesh):
    return jax.shard_map(
        local,
        mesh=mesh,
        in_specs=(
            P(("groups", "seq"), "chan"),
            P(("groups", "seq"), None),
            P(None, "chan"),
            P(None, "chan"),
            P(None, "chan"),
            P(None, None, "chan", None),
            P(None, "chan"),
            P(None, "chan"),
            P(None, None, "chan"),
            P(None, "chan"),
        ),
        out_specs=P(("groups", "seq"), "chan"),
        check_vma=False,
    )
```

```python
import jax
import jax.numpy as jnp
from jax import lax
from jax.experimental import pallas as pl
from jax.experimental.pallas import tpu as pltpu
from jax.sharding import PartitionSpec as P


D0 = 32
D1 = 48
HALO = D0 + D1
EXTRA = 16
BF = jnp.bfloat16
F32 = jnp.float32
VM = pl.BlockSpec(memory_space=pltpu.VMEM)
HBM = pl.BlockSpec(memory_space=pltpu.HBM)
GRANT = 14 << 20


def call(kernel, outs, hbm, vmem, scratch=(), grant=GRANT):
    hbm = [pltpu.with_memory_space_constraint(a, pltpu.HBM) for a in hbm]
    vmem = [pltpu.with_memory_space_constraint(a, pltpu.VMEM) for a in vmem]
    return pl.pallas_call(
        kernel,
        out_shape=[pltpu.VMEM(shape, dtype) for shape, dtype in outs],
        in_specs=[HBM] * len(hbm) + [VM] * len(vmem),
        out_specs=[VM] * len(outs),
        scratch_shapes=list(scratch),
        compiler_params=pltpu.CompilerParams(vmem_limit_bytes=grant),
    )(*hbm, *vmem)


def gelu(v):
    inner = v * (0.7978845608028654 + 0.035677408136300125 * (v * v))
    half = 0.5 * v
    return half + half * jnp.tanh(inner)


def dot(a, b):
    return jnp.dot(a, b, preferred_element_type=F32)


def tiles(start, stop, step):
    return [(i, min(step, stop - i)) for i in range(start, stop, step)]


def act_rows(x, s_ref, b_ref, layer):
    return gelu(x.astype(F32) * s_ref[layer : layer + 1] + b_ref[layer : layer + 1]).astype(BF)


def conv_rows(h_ref, base, spread, n, w_ref):
    lhs = jnp.concatenate(
        [h_ref[base + k * spread : base + k * spread + n] for k in (-1, 0, 1)], axis=1
    )
    return dot(lhs, w_ref[...])


def mid_rows(own, other, mid_ref, layer):
    u = own.astype(F32) + other.astype(F32)
    return gelu(u * mid_ref[layer : layer + 1] + mid_ref[2 + layer : 3 + layer]).astype(BF)


def embed_first(a_lo, a_hi, rows, width):
    def kernel(
        tower, dna, embed, ins, inb, conv_w, mids, midb, point_w,
        x0, h0, e_a, e_b, pa, w0, pw0, w1, s_in, b_in, own_mid,
        tower_v, dna_v, embed_v, mids_v, midb_v, sem,
    ):
        cp = pltpu.make_async_copy
        half = rows // 2
        c_dna = cp(dna, dna_v, sem.at[0])
        c_emb = cp(embed, embed_v, sem.at[1])
        c_tow = [
            cp(tower.at[pl.ds(i * half, half)], tower_v.at[pl.ds(i * half, half)], sem.at[2 + i])
            for i in range(2)
        ]
        c_s = cp(ins, s_in, sem.at[4])
        c_b = cp(inb, b_in, sem.at[5])
        c_ms = cp(mids, mids_v, sem.at[6])
        c_mb = cp(midb, midb_v, sem.at[7])
        c_w0 = [
            cp(conv_w.at[0, k], w0.at[pl.ds(k * width, width)], sem.at[8 + k]) for k in range(3)
        ]
        c_pw = cp(point_w.at[0], pw0, sem.at[11])
        c_w1 = [
            cp(conv_w.at[1, k], w1.at[pl.ds(k * width, width)], sem.at[12 + k]) for k in range(3)
        ]
        for c in [c_dna, c_emb, *c_tow, c_s, c_b, c_ms, c_mb, *c_w0, c_pw, *c_w1]:
            c.start()
        slots = dna.shape[0]
        row = lax.broadcasted_iota(jnp.int32, (4 * slots, slots), 0)
        col = lax.broadcasted_iota(jnp.int32, (4 * slots, slots), 1)
        spread_map = jnp.where((row >> 2) == col, 1.0, 0.0).astype(BF)
        c_dna.wait()
        c_emb.wait()
        c_s.wait()
        c_b.wait()
        for i, n in tiles(0, rows, 128):
            if i % half == 0:
                c_tow[i // half].wait()
            code = (lax.broadcasted_iota(jnp.int32, (4 * slots, n), 0) & 3).astype(F32)
            base = dot(spread_map, dna_v[:, i : i + n].astype(F32).astype(BF))
            onehot = jnp.where(base == code, 1.0, 0.0).T.astype(BF)
            x = (tower_v[i : i + n].astype(F32) + dot(onehot, embed_v[...])).astype(BF)
            x0[i : i + n] = x
            h0[i : i + n] = act_rows(x, s_in, b_in, 0)
        even = lax.rem(lax.axis_index("seq"), 2) == 0
        low = x0[0:HALO]
        high = x0[rows - HALO : rows]
        e_a[...] = jnp.where(even, high, low)
        e_b[...] = jnp.where(even, low, high)
        c_ms.wait()
        c_mb.wait()
        first = lax.axis_index("chan") == 0
        mid = jnp.concatenate([mids_v[...], midb_v[...]], axis=0)
        mid = jnp.concatenate(
            [jnp.where(first, mid, 0.0), jnp.where(first, 0.0, mid)], axis=1
        )
        own_mid[...] = mid
        big = mid.astype(BF)
        rest = mid - big.astype(F32)
        middle = rest.astype(BF)
        small = (rest - middle.astype(F32)).astype(BF)
        pa[a_hi - a_lo : a_hi - a_lo + EXTRA] = jnp.concatenate(
            [big.astype(F32), middle.astype(F32), small.astype(F32), jnp.zeros_like(mid)], axis=0
        ).astype(BF)
        for c in c_w0:
            c.wait()
        for i, n in tiles(a_lo, a_hi, 256):
            pa[i - a_lo : i - a_lo + n] = conv_rows(h0, i, D0, n, w0).astype(BF)
        c_pw.wait()
        for c in c_w1:
            c.wait()

    return kernel


def first_rest(b_lo, b_hi):
    def kernel(point_w, pool_w, h0, w0, pb, pw1, pool, sem):
        copies = [
            pltpu.make_async_copy(point_w.at[1], pw1, sem.at[0]),
            pltpu.make_async_copy(pool_w, pool, sem.at[1]),
        ]
        for c in copies:
            c.start()
        for i, n in tiles(b_lo, b_hi, 224):
            pb[i - b_lo : i - b_lo + n] = conv_rows(h0, i, D0, n, w0).astype(BF)
        for c in copies:
            c.wait()

    return kernel


def first_edges(rows):
    def kernel(r_a, r_b, h0, w0, s_in, b_in, pe, lo, hi, ext):
        seq = lax.axis_index("seq")
        even = lax.rem(seq, 2) == 0
        low = jnp.where(even, r_b[...], r_a[...])
        high = jnp.where(even, r_a[...], r_b[...])
        lo[...] = low
        hi[...] = high
        zero = jnp.zeros(low.shape, BF)
        inner = 2 * D0
        span = HALO + inner
        ext[0:HALO] = jnp.where(seq == 0, zero, act_rows(low, s_in, b_in, 0))
        ext[HALO:span] = h0[0:inner]
        ext[span : span + inner] = h0[rows - inner : rows]
        ext[span + inner : 2 * span] = jnp.where(
            seq == lax.axis_size("seq") - 1, zero, act_rows(high, s_in, b_in, 0)
        )
        lhs = [
            jnp.concatenate(
                [ext[s + k * D0 : s + k * D0 + HALO] for k in range(3)], axis=1
            )
            for s in (0, span)
        ]
        pe[...] = dot(jnp.concatenate(lhs, axis=0), w0[...]).astype(BF)

    return kernel


def second_first(a_lo, a_hi, c_lo, c_hi):
    def kernel(pa, ra, x0, pw0, w1, s_in, b_in, own_mid, x1a, h1a, qa, mid):
        n_a = a_hi - a_lo
        tail = ra[n_a : n_a + EXTRA].astype(F32)
        mid[...] = own_mid[...] + (tail[0:4] + tail[4:8] + tail[8:12])
        for i, n in tiles(0, n_a, 256):
            z = mid_rows(pa[i : i + n], ra[i : i + n], mid, 0)
            x = (x0[a_lo + i : a_lo + i + n].astype(F32) + dot(z, pw0[...])).astype(BF)
            x1a[i : i + n] = x
            h1a[i : i + n] = act_rows(x, s_in, b_in, 1)
        for i, n in tiles(c_lo, c_hi, 192):
            qa[i - c_lo : i - c_lo + n] = conv_rows(h1a, i - a_lo, D1, n, w1).astype(BF)

    return kernel


def second_rest(rows, a_lo, a_hi, c_hi, e_hi):
    def kernel(pb, rb, x0, x1a, h1a, pw0, w1, mid, s_in, b_in, x1b, x1t, h1t, qb, h1):
        b_hi = rows - D0
        first = c_hi - D1
        h1[0 : a_hi - first] = h1a[first - a_lo : a_hi - a_lo]
        x1b[0 : a_hi - c_hi] = x1a[c_hi - a_lo : a_hi - a_lo]
        for i, n in tiles(0, b_hi - a_hi, 224):
            z = mid_rows(pb[i : i + n], rb[i : i + n], mid, 0)
            g = a_hi + i
            x = (x0[g : g + n].astype(F32) + dot(z, pw0[...])).astype(BF)
            h1[g - first : g - first + n] = act_rows(x, s_in, b_in, 1)
            keep = min(n, e_hi - g)
            x1b[g - c_hi : g - c_hi + keep] = x[0:keep]
            if keep < n:
                x1t[...] = x[keep:]
        h1t[...] = h1[e_hi - D1 - first : b_hi - first]
        for i, n in tiles(c_hi, e_hi, 224):
            qb[i - c_hi : i - c_hi + n] = conv_rows(h1, i - first, D1, n, w1).astype(BF)

    return kernel


def second_edges(rows, a_lo, c_lo, e_hi):
    def kernel(pe, re, x0, lo, hi, x1a, h1a, x1t, h1t, pw0, w1, mid, s_in, b_in, x1c, qc, ext):
        seq = lax.axis_index("seq")
        z = mid_rows(pe[...], re[...], mid, 0)
        base = jnp.concatenate(
            [lo[HALO - D1 : HALO], x0[0:D0], x0[rows - D0 : rows], hi[0:D1]], axis=0
        )
        x = (base.astype(F32) + dot(z, pw0[...])).astype(BF)
        tail = rows - D0 - e_hi
        x1c[0:D0] = x[D1 : D1 + D0]
        x1c[D0:c_lo] = x1a[0 : c_lo - a_lo]
        x1c[c_lo : c_lo + tail] = x1t[...]
        x1c[c_lo + tail : c_lo + tail + D0] = x[HALO : HALO + D0]
        h = act_rows(x, s_in, b_in, 1)
        zero = jnp.zeros((D1, h.shape[1]), BF)
        top = c_lo + 2 * D1
        bottom = rows - e_hi + 2 * D1
        ext[0:D1] = jnp.where(seq == 0, zero, h[0:D1])
        ext[D1:HALO] = h[D1:HALO]
        ext[HALO:top] = h1a[0 : c_lo + D1 - a_lo]
        ext[top : top + bottom - HALO] = h1t[...]
        ext[top + bottom - HALO : top + bottom - D1] = h[HALO : HALO + D0]
        ext[top + bottom - D1 : top + bottom] = jnp.where(
            seq == lax.axis_size("seq") - 1, zero, h[HALO + D0 :]
        )
        lhs = [
            jnp.concatenate([ext[s + k * D1 : s + k * D1 + n] for k in range(3)], axis=1)
            for s, n in ((0, c_lo), (top, rows - e_hi))
        ]
        qc[...] = dot(jnp.concatenate(lhs, axis=0), w1[...]).astype(BF)

    return kernel


def last_point(x_base, n_rows, step):
    def kernel(q, r, x1, pw1, mid, dm, df, xo, wide):
        for i, n in tiles(0, n_rows, step):
            z = mid_rows(q[i : i + n], r[i : i + n], mid, 1)
            x = x1[x_base + i : x_base + i + n].astype(F32) + dot(z, pw1[...])
            x = x.astype(BF).astype(F32)
            j, m = i // 2, n // 2
            for k in range(wide.shape[0]):
                cols = slice(128 * k, 128 * (k + 1))
                wide[k, i : i + n] = x[:, cols]
                first = wide[k, pl.ds(i, m, stride=2), :]
                second = wide[k, pl.ds(i + 1, m, stride=2), :]
                d = first - second
                dm[j : j + m, cols] = d.astype(BF)
                df[j : j + m, cols] = d
                xo[j : j + m, cols] = second.astype(BF)

    return kernel


def pool_first(da, ra, db, rb, dc, pool, dfa, xoa, dfb, xob, ya, yb, lc):
    width = da.shape[1]
    chan = lax.axis_index("chan")
    mine = pl.ds(pl.multiple_of(chan * width, 128), width)
    theirs = pl.ds(pl.multiple_of((1 - chan) * width, 128), width)
    lc[...] = dot(dc[...], pool[mine, :])
    for d, r, df, xo, y in ((da, ra, dfa, xoa, ya), (db, rb, dfb, xob, yb)):
        logit = dot(d[...], pool[mine, :]) + dot(r[...], pool[theirs, :])
        y[...] = (xo[...].astype(F32) + jax.nn.sigmoid(logit) * df[...]).astype(BF)


def pool_last(p_lo, p_hi, p_end):
    def kernel(rc, lc, pool, dfc, xoc, ya, yb, out, y, sem):
        width = rc.shape[1]
        chan = lax.axis_index("chan")
        theirs = pl.ds(pl.multiple_of((1 - chan) * width, 128), width)
        copy = pltpu.make_async_copy
        last = rc.shape[0] - p_lo
        copies = [
            copy(ya, out.at[pl.ds(p_lo, p_hi - p_lo)], sem.at[0]),
            copy(yb, out.at[pl.ds(p_hi, p_end - p_hi)], sem.at[1]),
            copy(y.at[pl.ds(0, p_lo)], out.at[pl.ds(0, p_lo)], sem.at[2]),
            copy(y.at[pl.ds(p_lo, last)], out.at[pl.ds(p_end, last)], sem.at[3]),
        ]
        copies[0].start()
        copies[1].start()
        logit = lc[...] + dot(rc[...], pool[theirs, :])
        y[...] = (xoc[...].astype(F32) + jax.nn.sigmoid(logit) * dfc[...]).astype(BF)
        copies[2].start()
        copies[3].start()
        for c in copies:
            c.wait()

    return kernel


def swap_chan(a):
    return lax.ppermute(a, "chan", [(0, 1), (1, 0)])


def local(
    tower_input, dna_bases, base_embed, in_scale, entry_norm_shift,
    conv_w, mid_scale, mid_shift, point_w, pooling_weight,
):
    rows, width = tower_input.shape
    inner = conv_w.shape[3]
    a_lo, a_hi = D0, rows // 2 + 32
    c_lo, c_hi, e_hi = 96, rows // 2 - 32, rows - 96
    b_hi = rows - D0
    n_a, n_b = a_hi - a_lo, b_hi - a_hi
    m_a, m_b = c_hi - c_lo, e_hi - c_hi
    m_c = rows - m_a - m_b
    dma = pltpu.SemaphoreType.DMA
    x0, h0, e_a, e_b, pa, w0, pw0, w1, s_in, b_in, own_mid = call(
        embed_first(a_lo, a_hi, rows, width),
        [
            ((rows, width), BF), ((rows, width), BF), ((HALO, width), BF), ((HALO, width), BF),
            ((n_a + EXTRA, inner), BF), ((3 * width, inner), BF), ((inner, width), BF),
            ((3 * width, inner), BF), ((2, width), F32), ((2, width), F32), ((4, inner), F32),
        ],
        [
            tower_input, dna_bases.T, base_embed, in_scale, entry_norm_shift, conv_w,
            mid_scale, mid_shift, point_w,
        ],
        [],
        [
            pltpu.VMEM((rows, width), BF), pltpu.VMEM(dna_bases.shape[::-1], jnp.int32),
            pltpu.VMEM(base_embed.shape, BF), pltpu.VMEM(mid_scale.shape, F32),
            pltpu.VMEM(mid_shift.shape, F32), dma((15,)),
        ],
    )
    ra = swap_chan(pa)
    count = lax.axis_size("seq")
    pairs_a = [(i, i ^ 1) for i in range(count)]
    pairs_b = [(i, ((i - 1) ^ 1) + 1) for i in range(1, count - 1)]
    r_a = lax.ppermute(e_a, "seq", pairs_a)
    r_b = lax.ppermute(e_b, "seq", pairs_b)
    pb, pw1, pool = call(
        first_rest(a_hi, b_hi),
        [((n_b, inner), BF), ((inner, width), BF), (pooling_weight.shape, BF)],
        [point_w, pooling_weight],
        [h0, w0],
        [dma((2,))],
    )
    rb = swap_chan(pb)
    x1a, h1a, qa, mid = call(
        second_first(a_lo, a_hi, c_lo, c_hi),
        [((n_a, width), BF), ((n_a, width), BF), ((m_a, inner), BF), ((4, inner), F32)],
        [],
        [pa, ra, x0, pw0, w1, s_in, b_in, own_mid],
    )
    sa = swap_chan(qa)
    pe, lo, hi = call(
        first_edges(rows),
        [((2 * HALO, inner), BF), ((HALO, width), BF), ((HALO, width), BF)],
        [],
        [r_a, r_b, h0, w0, s_in, b_in],
        [pltpu.VMEM((2 * (HALO + 2 * D0), width), BF)],
    )
    re = swap_chan(pe)
    x1b, x1t, h1t, qb = call(
        second_rest(rows, a_lo, a_hi, c_hi, e_hi),
        [
            ((m_b, width), BF), ((b_hi - e_hi, width), BF),
            ((b_hi - e_hi + D1, width), BF), ((m_b, inner), BF),
        ],
        [],
        [pb, rb, x0, x1a, h1a, pw0, w1, mid, s_in, b_in],
        [pltpu.VMEM((b_hi - c_hi + D1, width), BF)],
    )
    sb = swap_chan(qb)
    x1c, qc = call(
        second_edges(rows, a_lo, c_lo, e_hi),
        [((m_c, width), BF), ((m_c, inner), BF)],
        [],
        [pe, re, x0, lo, hi, x1a, h1a, x1t, h1t, pw0, w1, mid, s_in, b_in],
        [pltpu.VMEM((m_c + 4 * D1, width), BF)],
    )
    sc = swap_chan(qc)
    ends = []
    for q, s, x1, base, m, step in (
        (qa, sa, x1a, c_lo - a_lo, m_a, 128), (qb, sb, x1b, 0, m_b, 128), (qc, sc, x1c, 0, m_c, 96)
    ):
        dm, df, xo = call(
            last_point(base, m, step),
            [((m // 2, width), BF), ((m // 2, width), F32), ((m // 2, width), BF)],
            [],
            [q, s, x1, pw1, mid],
            [pltpu.VMEM((width // 128, m, 128), F32)],
        )
        ends.append((dm, swap_chan(dm), df, xo))
    (da, ta, dfa, xoa), (db, tb, dfb, xob), (dc, tc, dfc, xoc) = ends
    ya, yb, lc = call(
        pool_first,
        [((m_a // 2, width), BF), ((m_b // 2, width), BF), ((m_c // 2, width), F32)],
        [],
        [da, ta, db, tb, dc, pool, dfa, xoa, dfb, xob],
    )
    vm = [
        pltpu.with_memory_space_constraint(a, pltpu.VMEM)
        for a in (tc, lc, pool, dfc, xoc, ya, yb)
    ]
    return pl.pallas_call(
        pool_last(c_lo // 2, c_hi // 2, e_hi // 2),
        out_shape=jax.ShapeDtypeStruct((rows // 2, width), BF),
        in_specs=[VM] * 7,
        out_specs=HBM,
        scratch_shapes=[pltpu.VMEM((m_c // 2, width), BF), dma((4,))],
        compiler_params=pltpu.CompilerParams(vmem_limit_bytes=GRANT),
    )(*vm)


def solution(mesh):
    return jax.shard_map(
        local,
        mesh=mesh,
        in_specs=(
            P(("groups", "seq"), "chan"),
            P(("groups", "seq"), None),
            P(None, "chan"),
            P(None, "chan"),
            P(None, "chan"),
            P(None, None, "chan", None),
            P(None, "chan"),
            P(None, "chan"),
            P(None, None, "chan"),
            P(None, "chan"),
        ),
        out_specs=P(("groups", "seq"), "chan"),
        check_vma=False,
    )
```

```python
import jax
import jax.numpy as jnp
from jax import lax
from jax.experimental import pallas as pl
from jax.experimental.pallas import tpu as pltpu
from jax.sharding import PartitionSpec as P


D0 = 32
D1 = 48
HALO = D0 + D1
EXTRA = 16
PIECE = 32
BF = jnp.bfloat16
F32 = jnp.float32
VM = pl.BlockSpec(memory_space=pltpu.VMEM)
HBM = pl.BlockSpec(memory_space=pltpu.HBM)
GRANT = 14 << 20


def call(kernel, outs, hbm, vmem, scratch=(), grant=GRANT):
    hbm = [pltpu.with_memory_space_constraint(a, pltpu.HBM) for a in hbm]
    vmem = [pltpu.with_memory_space_constraint(a, pltpu.VMEM) for a in vmem]
    return pl.pallas_call(
        kernel,
        out_shape=[pltpu.VMEM(shape, dtype) for shape, dtype in outs],
        in_specs=[HBM] * len(hbm) + [VM] * len(vmem),
        out_specs=[VM] * len(outs),
        scratch_shapes=list(scratch),
        compiler_params=pltpu.CompilerParams(vmem_limit_bytes=grant),
    )(*hbm, *vmem)


def gelu(v):
    inner = v * (BF(0.7978845608028654) + BF(0.035677408136300125) * (v * v))
    half = BF(0.5) * v
    return half + half * jnp.tanh(inner)


def dot(a, b):
    return jnp.dot(a, b, preferred_element_type=F32)


def tiles(start, stop, step):
    return [(i, min(step, stop - i)) for i in range(start, stop, step)]


def act_rows(x, s_ref, b_ref, layer):
    return gelu(x * s_ref[layer : layer + 1].astype(BF) + b_ref[layer : layer + 1].astype(BF))


def taps(h_ref, base, spread, n):
    return jnp.concatenate(
        [h_ref[base + k * spread : base + k * spread + n] for k in (-1, 0, 1)], axis=1
    )


def put_mid(z_ref, own, other, mid_ref, layer, start, n):
    for i, m in tiles(start, start + n, PIECE):
        scale = mid_ref[layer : layer + 1].astype(BF)
        z_ref[i : i + m] = gelu(
            (own[i : i + m] + other[i : i + m]) * scale
            + mid_ref[2 + layer : 3 + layer].astype(BF)
        )


def sigmoid(v):
    return 0.5 + 0.5 * jnp.tanh(0.5 * v)


def embed_first(a_lo, a_hi, rows, width):
    def kernel(
        tower, dna, embed, ins, inb, conv_w, mids, midb, point_w,
        x0, h0, e_a, e_b, pa, w0, pw0, s_in, b_in, own_mid,
        tower_v, dna_v, embed_v, mids_v, midb_v, codes, emb, sem,
    ):
        cp = pltpu.make_async_copy
        step = 128
        quarter = rows // 4
        c_dna = cp(dna, dna_v, sem.at[0])
        c_emb = cp(embed, embed_v, sem.at[1])
        c_tow = [
            cp(
                tower.at[pl.ds(i * quarter, quarter)],
                tower_v.at[pl.ds(i * quarter, quarter)],
                sem.at[2 + i],
            )
            for i in range(4)
        ]
        c_small = [
            cp(ins, s_in, sem.at[6]), cp(inb, b_in, sem.at[7]),
            cp(mids, mids_v, sem.at[8]), cp(midb, midb_v, sem.at[9]),
        ]
        c_w0 = [
            cp(conv_w.at[0, k], w0.at[pl.ds(k * width, width)], sem.at[10 + k]) for k in range(3)
        ]
        c_pw = cp(point_w.at[0], pw0, sem.at[13])
        for c in [c_dna, c_emb, c_small[0], c_small[1], *c_tow, *c_small[2:]]:
            c.start()
        slots = dna.shape[0]
        row = lax.broadcasted_iota(jnp.int32, (4 * slots, slots), 0)
        col = lax.broadcasted_iota(jnp.int32, (4 * slots, slots), 1)
        spread_map = jnp.where((row >> 2) == col, 1.0, 0.0).astype(BF)
        code = (lax.broadcasted_iota(jnp.int32, (4 * slots, step), 0) & 3).astype(F32)
        c_dna.wait()
        c_w0[0].start()
        for i, n in tiles(0, rows, step):
            base = dot(spread_map, dna_v[:, i : i + n].astype(F32).astype(BF))
            codes[i : i + n] = jnp.where(base == code, 1.0, 0.0).T.astype(BF)
        c_emb.wait()
        c_small[0].wait()
        c_small[1].wait()
        c_w0[1].start()
        c_w0[2].start()
        c_pw.start()

        def embed_tile(i, n):
            emb[i : i + n] = dot(codes[i : i + n], embed_v[...])

        def act_tile(start, n):
            for i, m in tiles(start, start + n, PIECE):
                x = (tower_v[i : i + m].astype(F32) + emb[i : i + m]).astype(BF)
                x0[i : i + m] = x
                h0[i : i + m] = act_rows(x, s_in, b_in, 0)

        work = tiles(0, rows, step)
        embed_tile(*work[0])
        need = -(-(a_hi + D0) // step)
        for t in range(need):
            i, n = work[t]
            if i % quarter == 0:
                c_tow[i // quarter].wait()
            if t + 1 < len(work):
                embed_tile(*work[t + 1])
            act_tile(i, n)
        for q in range(-(-need * step // quarter), 4):
            c_tow[q].wait()
        for t in range(need, len(work)):
            if t + 1 < len(work):
                embed_tile(*work[t + 1])
            act_tile(*work[t])
        for k in range(3):
            c_w0[k].wait()
        for i, n in tiles(a_lo, a_hi, 512):
            pa[i - a_lo : i - a_lo + n] = dot(taps(h0, i, D0, n), w0[...]).astype(BF)
        even = lax.rem(lax.axis_index("seq"), 2) == 0
        low = x0[0:HALO]
        high = x0[rows - HALO : rows]
        e_a[...] = jnp.where(even, high, low)
        e_b[...] = jnp.where(even, low, high)
        c_small[2].wait()
        c_small[3].wait()
        first = lax.axis_index("chan") == 0
        mid = jnp.concatenate([mids_v[...], midb_v[...]], axis=0)
        mid = jnp.concatenate(
            [jnp.where(first, mid, 0.0), jnp.where(first, 0.0, mid)], axis=1
        )
        own_mid[...] = mid
        big = mid.astype(BF)
        rest = mid - big.astype(F32)
        middle = rest.astype(BF)
        small = (rest - middle.astype(F32)).astype(BF)
        pa[a_hi - a_lo : a_hi - a_lo + EXTRA] = jnp.concatenate(
            [big.astype(F32), middle.astype(F32), small.astype(F32), jnp.zeros_like(mid)], axis=0
        ).astype(BF)
        c_pw.wait()

    return kernel


def first_rest(b_lo, b_hi):
    def kernel(conv_w, h0, w0, pb, w1, sem):
        width = w0.shape[1]
        copies = [
            pltpu.make_async_copy(conv_w.at[1, k], w1.at[pl.ds(k * width, width)], sem.at[k])
            for k in range(3)
        ]
        for c in copies:
            c.start()
        for i, n in tiles(b_lo, b_hi, b_hi - b_lo):
            pb[i - b_lo : i - b_lo + n] = dot(taps(h0, i, D0, n), w0[...]).astype(BF)
        for c in copies:
            c.wait()

    return kernel


def first_edges(rows):
    def kernel(r_a, r_b, h0, w0, s_in, b_in, pe, lo, hi, ext):
        seq = lax.axis_index("seq")
        even = lax.rem(seq, 2) == 0
        inner = 2 * D0
        span = HALO + inner
        ext[HALO:span] = h0[0:inner]
        ext[span : span + inner] = h0[rows - inner : rows]
        ends = (
            (lo, r_b, r_a, 0, seq == 0),
            (hi, r_a, r_b, span + inner, seq == lax.axis_size("seq") - 1),
        )
        for i, m in tiles(0, HALO, PIECE):
            zero = jnp.zeros((m, h0.shape[1]), BF)
            for keep, at_even, at_odd, at, outside in ends:
                x = jnp.where(even, at_even[i : i + m], at_odd[i : i + m])
                keep[i : i + m] = x
                ext[at + i : at + i + m] = jnp.where(outside, zero, act_rows(x, s_in, b_in, 0))
        lhs = [taps(ext, s + D0, D0, HALO) for s in (0, span)]
        pe[...] = dot(jnp.concatenate(lhs, axis=0), w0[...]).astype(BF)

    return kernel


def second_first(a_lo, a_hi, c_lo, c_hi):
    def kernel(
        point_w, pool_w, pa, ra, x0, pw0, w1, s_in, b_in, own_mid,
        x1a, h1a, qa, mid, pw1, pool, z, acc, sem,
    ):
        copies = [
            pltpu.make_async_copy(point_w.at[1], pw1, sem.at[0]),
            pltpu.make_async_copy(pool_w, pool, sem.at[1]),
        ]
        for c in copies:
            c.start()
        step = 128
        n_a = a_hi - a_lo
        tail = ra[n_a : n_a + EXTRA].astype(F32)
        mid[...] = own_mid[...] + (tail[0:4] + tail[4:8] + tail[8:12])
        work = tiles(0, n_a, step)
        convs = tiles(c_lo, c_hi, step)

        def act_tile(start, n):
            for i, m in tiles(start, start + n, PIECE):
                x = (x0[a_lo + i : a_lo + i + m].astype(F32) + acc[i : i + m]).astype(BF)
                x1a[i : i + m] = x
                h1a[i : i + m] = act_rows(x, s_in, b_in, 1)

        put_mid(z, pa, ra, mid, 0, *work[0])
        for t in range(len(work) + 2 + len(convs)):
            if t + 1 < len(work):
                put_mid(z, pa, ra, mid, 0, *work[t + 1])
            if 1 <= t <= len(work):
                act_tile(*work[t - 1])
            if t < len(work):
                i, n = work[t]
                acc[i : i + n] = dot(z[i : i + n], pw0[...])
            if convs and sum(convs[0]) + D1 - a_lo <= (t - 1) * step:
                i, n = convs.pop(0)
                qa[i - c_lo : i - c_lo + n] = dot(taps(h1a, i - a_lo, D1, n), w1[...]).astype(BF)
        assert not convs
        for c in copies:
            c.wait()

    return kernel


def second_rest(rows, a_lo, a_hi, c_hi, e_hi):
    def kernel(
        pb, rb, x0, x1a, h1a, pw0, w1, mid, s_in, b_in, x1b, x1t, h1t, qb, h1, z, acc
    ):
        step = 224
        b_hi = rows - D0
        first = c_hi - D1
        h1[0 : a_hi - first] = h1a[first - a_lo : a_hi - a_lo]
        x1b[0 : a_hi - c_hi] = x1a[c_hi - a_lo : a_hi - a_lo]
        work = tiles(0, b_hi - a_hi, step)
        convs = tiles(c_hi, e_hi, step)

        def act_tile(start, n):
            for i, m in tiles(start, start + n, PIECE):
                g = a_hi + i
                x = (x0[g : g + m].astype(F32) + acc[i : i + m]).astype(BF)
                h1[g - first : g - first + m] = act_rows(x, s_in, b_in, 1)
                keep = max(0, min(m, e_hi - g))
                if keep:
                    x1b[g - c_hi : g - c_hi + keep] = x[0:keep]
                if keep < m:
                    x1t[g + keep - e_hi : g + m - e_hi] = x[keep:]

        put_mid(z, pb, rb, mid, 0, *work[0])
        for t in range(len(work) + 2 + len(convs)):
            if t + 1 < len(work):
                put_mid(z, pb, rb, mid, 0, *work[t + 1])
            if 1 <= t <= len(work):
                act_tile(*work[t - 1])
            if t < len(work):
                i, n = work[t]
                acc[i : i + n] = dot(z[i : i + n], pw0[...])
            if t >= 2 and convs:
                i, n = convs.pop(0)
                qb[i - c_hi : i - c_hi + n] = dot(taps(h1, i - first, D1, n), w1[...]).astype(BF)
        h1t[...] = h1[e_hi - D1 - first : b_hi - first]

    return kernel


def second_edges(rows, a_lo, c_lo, e_hi):
    def kernel(
        pe, re, x0, lo, hi, x1a, h1a, x1t, h1t, pw0, w1, mid, s_in, b_in, x1c, qc, ext, z, acc
    ):
        seq = lax.axis_index("seq")
        tail = rows - D0 - e_hi
        top = c_lo + 2 * D1
        bottom = rows - e_hi + 2 * D1
        put_mid(z, pe, re, mid, 0, 0, 2 * HALO)
        acc[...] = dot(z[...], pw0[...])
        x1c[D0:c_lo] = x1a[0 : c_lo - a_lo]
        x1c[c_lo : c_lo + tail] = x1t[...]
        ext[HALO:top] = h1a[0 : c_lo + D1 - a_lo]
        ext[top : top + bottom - HALO] = h1t[...]
        low = top + bottom - HALO
        parts = (
            (0, 32, lo, HALO - D1, 0, None, seq == 0),
            (32, 16, lo, HALO - 16, 32, None, seq == 0),
            (D1, D0, x0, 0, D1, 0, None),
            (HALO, D0, x0, rows - D0, low, c_lo + tail, None),
            (HALO + D0, 32, hi, 0, low + D0, None, seq == lax.axis_size("seq") - 1),
            (HALO + D0 + 32, 16, hi, 32, low + D0 + 32, None, seq == lax.axis_size("seq") - 1),
        )
        for i, m, base, at, to, keep, outside in parts:
            x = (base[at : at + m].astype(F32) + acc[i : i + m]).astype(BF)
            h = act_rows(x, s_in, b_in, 1)
            if keep is not None:
                x1c[keep : keep + m] = x
            if outside is not None:
                h = jnp.where(outside, jnp.zeros_like(h), h)
            ext[to : to + m] = h
        lhs = [taps(ext, s + D1, D1, n) for s, n in ((0, c_lo), (top, rows - e_hi))]
        qc[...] = dot(jnp.concatenate(lhs, axis=0), w1[...]).astype(BF)

    return kernel


def own_half(width):
    chan = lax.axis_index("chan")
    mine = pl.ds(pl.multiple_of(chan * width, 128), width)
    theirs = pl.ds(pl.multiple_of((1 - chan) * width, 128), width)
    return mine, theirs


def last_point(x_base, n_rows, step, has_pool):
    def kernel(q, r, x1, pw1, mid, *rest):
        if has_pool:
            d_prev, pool, dm, df, xo, l_prev, z, acc, wide = rest
        else:
            dm, df, xo, z, acc, wide = rest

        def tail(start, n):
            for i, m in tiles(start, start + n, PIECE):
                x = x1[x_base + i : x_base + i + m].astype(F32) + acc[i : i + m]
                x = x.astype(BF).astype(F32)
                j, half = i // 2, m // 2
                firsts, seconds = [], []
                for k in range(wide.shape[0]):
                    wide[k, i : i + m] = x[:, 128 * k : 128 * (k + 1)]
                    firsts.append(wide[k, pl.ds(i, half, stride=2), :])
                    seconds.append(wide[k, pl.ds(i + 1, half, stride=2), :])
                second = jnp.concatenate(seconds, axis=1)
                d = jnp.concatenate(firsts, axis=1) - second
                dm[j : j + half] = d.astype(BF)
                df[j : j + half] = d
                xo[j : j + half] = second.astype(BF)

        work = tiles(0, n_rows, step)
        put_mid(z, q, r, mid, 1, *work[0])
        if has_pool:
            l_prev[...] = dot(d_prev[...], pool[own_half(pw1.shape[1])[0], :])
        for t in range(len(work) + 1):
            if t + 1 < len(work):
                put_mid(z, q, r, mid, 1, *work[t + 1])
            if t < len(work):
                i, n = work[t]
                acc[i : i + n] = dot(z[i : i + n], pw1[...])
            if t >= 1:
                tail(*work[t - 1])

    return kernel


def finish(y, xo, df, logit):
    for i, m in tiles(0, y.shape[0], PIECE):
        y[i : i + m] = (
            xo[i : i + m].astype(F32) + sigmoid(logit[i : i + m]) * df[i : i + m]
        ).astype(BF)


def pool_first(ra, la, rb, lb, dc, pool, dfa, xoa, dfb, xob, ya, yb, lc, acc_a, acc_b):
    mine, theirs = own_half(ra.shape[1])
    acc_a[...] = la[...] + dot(ra[...], pool[theirs, :])
    acc_b[...] = lb[...] + dot(rb[...], pool[theirs, :])
    finish(ya, xoa, dfa, acc_a)
    lc[...] = dot(dc[...], pool[mine, :])
    finish(yb, xob, dfb, acc_b)


def pool_last(p_lo, p_hi, p_end):
    def kernel(rc, lc, pool, dfc, xoc, ya, yb, out, y, acc, sem):
        theirs = own_half(rc.shape[1])[1]
        copy = pltpu.make_async_copy
        last = rc.shape[0] - p_lo
        copies = [
            copy(ya, out.at[pl.ds(p_lo, p_hi - p_lo)], sem.at[0]),
            copy(yb, out.at[pl.ds(p_hi, p_end - p_hi)], sem.at[1]),
            copy(y.at[pl.ds(0, p_lo)], out.at[pl.ds(0, p_lo)], sem.at[2]),
            copy(y.at[pl.ds(p_lo, last)], out.at[pl.ds(p_end, last)], sem.at[3]),
        ]
        copies[0].start()
        copies[1].start()
        acc[...] = lc[...] + dot(rc[...], pool[theirs, :])
        finish(y, xoc, dfc, acc)
        copies[2].start()
        copies[3].start()
        for c in copies:
            c.wait()

    return kernel


def swap_chan(a):
    return lax.ppermute(a, "chan", [(0, 1), (1, 0)])


def local(
    tower_input, dna_bases, base_embed, in_scale, entry_norm_shift,
    conv_w, mid_scale, mid_shift, point_w, pooling_weight,
):
    rows, width = tower_input.shape
    inner = conv_w.shape[3]
    a_lo, a_hi = D0, rows // 2 + 32
    c_lo, c_hi, e_hi = 96, rows // 2 - 32, rows - 96
    b_hi = rows - D0
    n_a, n_b = a_hi - a_lo, b_hi - a_hi
    m_a, m_b = c_hi - c_lo, e_hi - c_hi
    m_c = rows - m_a - m_b
    dma = pltpu.SemaphoreType.DMA
    x0, h0, e_a, e_b, pa, w0, pw0, s_in, b_in, own_mid = call(
        embed_first(a_lo, a_hi, rows, width),
        [
            ((rows, width), BF), ((rows, width), BF), ((HALO, width), BF), ((HALO, width), BF),
            ((n_a + EXTRA, inner), BF), ((3 * width, inner), BF), ((inner, width), BF),
            ((2, width), F32), ((2, width), F32), ((4, inner), F32),
        ],
        [
            tower_input, dna_bases.T, base_embed, in_scale, entry_norm_shift, conv_w,
            mid_scale, mid_shift, point_w,
        ],
        [],
        [
            pltpu.VMEM((rows, width), BF), pltpu.VMEM(dna_bases.shape[::-1], jnp.int32),
            pltpu.VMEM(base_embed.shape, BF), pltpu.VMEM(mid_scale.shape, F32),
            pltpu.VMEM(mid_shift.shape, F32), pltpu.VMEM((rows, 4 * dna_bases.shape[1]), BF),
            pltpu.VMEM((rows, width), F32), dma((14,)),
        ],
    )
    ra = swap_chan(pa)
    count = lax.axis_size("seq")
    pairs_a = [(i, i ^ 1) for i in range(count)]
    pairs_b = [(i, ((i - 1) ^ 1) + 1) for i in range(1, count - 1)]
    r_a = lax.ppermute(e_a, "seq", pairs_a)
    r_b = lax.ppermute(e_b, "seq", pairs_b)
    pb, w1 = call(
        first_rest(a_hi, b_hi),
        [((n_b, inner), BF), ((3 * width, inner), BF)],
        [conv_w],
        [h0, w0],
        [dma((3,))],
    )
    rb = swap_chan(pb)
    x1a, h1a, qa, mid, pw1, pool = call(
        second_first(a_lo, a_hi, c_lo, c_hi),
        [
            ((n_a, width), BF), ((n_a, width), BF), ((m_a, inner), BF), ((4, inner), F32),
            ((inner, width), BF), (pooling_weight.shape, BF),
        ],
        [point_w, pooling_weight],
        [pa, ra, x0, pw0, w1, s_in, b_in, own_mid],
        [pltpu.VMEM((n_a, inner), BF), pltpu.VMEM((n_a, width), F32), dma((2,))],
    )
    sa = swap_chan(qa)
    pe, lo, hi = call(
        first_edges(rows),
        [((2 * HALO, inner), BF), ((HALO, width), BF), ((HALO, width), BF)],
        [],
        [r_a, r_b, h0, w0, s_in, b_in],
        [pltpu.VMEM((2 * (HALO + 2 * D0), width), BF)],
    )
    re = swap_chan(pe)
    x1b, x1t, h1t, qb = call(
        second_rest(rows, a_lo, a_hi, c_hi, e_hi),
        [
            ((m_b, width), BF), ((b_hi - e_hi, width), BF),
            ((b_hi - e_hi + D1, width), BF), ((m_b, inner), BF),
        ],
        [],
        [pb, rb, x0, x1a, h1a, pw0, w1, mid, s_in, b_in],
        [
            pltpu.VMEM((b_hi - c_hi + D1, width), BF), pltpu.VMEM((n_b, inner), BF),
            pltpu.VMEM((n_b, width), F32),
        ],
    )
    sb = swap_chan(qb)
    x1c, qc = call(
        second_edges(rows, a_lo, c_lo, e_hi),
        [((m_c, width), BF), ((m_c, inner), BF)],
        [],
        [pe, re, x0, lo, hi, x1a, h1a, x1t, h1t, pw0, w1, mid, s_in, b_in],
        [
            pltpu.VMEM((m_c + 4 * D1, width), BF), pltpu.VMEM((2 * HALO, inner), BF),
            pltpu.VMEM((2 * HALO, width), F32),
        ],
    )
    sc = swap_chan(qc)
    ends, halves = [], []
    for q, s, x1, base, m, step in (
        (qa, sa, x1a, c_lo - a_lo, m_a, 128), (qb, sb, x1b, 0, m_b, 128), (qc, sc, x1c, 0, m_c, 96)
    ):
        before = [ends[-1][0], pool] if ends else []
        dm, df, xo, *half = call(
            last_point(base, m, step, bool(before)),
            [((m // 2, width), BF), ((m // 2, width), F32), ((m // 2, width), BF)]
            + [((d.shape[0], width), F32) for d in before[:1]],
            [],
            [q, s, x1, pw1, mid, *before],
            [
                pltpu.VMEM((m, inner), BF), pltpu.VMEM((m, width), F32),
                pltpu.VMEM((width // 128, m, 128), F32),
            ],
        )
        halves += half
        ends.append((dm, swap_chan(dm), df, xo))
    (da, ta, dfa, xoa), (db, tb, dfb, xob), (dc, tc, dfc, xoc) = ends
    la, lb = halves
    ya, yb, lc = call(
        pool_first,
        [((m_a // 2, width), BF), ((m_b // 2, width), BF), ((m_c // 2, width), F32)],
        [],
        [ta, la, tb, lb, dc, pool, dfa, xoa, dfb, xob],
        [pltpu.VMEM((m_a // 2, width), F32), pltpu.VMEM((m_b // 2, width), F32)],
    )
    vm = [
        pltpu.with_memory_space_constraint(a, pltpu.VMEM)
        for a in (tc, lc, pool, dfc, xoc, ya, yb)
    ]
    return pl.pallas_call(
        pool_last(c_lo // 2, c_hi // 2, e_hi // 2),
        out_shape=jax.ShapeDtypeStruct((rows // 2, width), BF),
        in_specs=[VM] * 7,
        out_specs=HBM,
        scratch_shapes=[
            pltpu.VMEM((m_c // 2, width), BF), pltpu.VMEM((m_c // 2, width), F32), dma((4,)),
        ],
        compiler_params=pltpu.CompilerParams(vmem_limit_bytes=GRANT),
    )(*vm)


def solution(mesh):
    return jax.shard_map(
        local,
        mesh=mesh,
        in_specs=(
            P(("groups", "seq"), "chan"),
            P(("groups", "seq"), None),
            P(None, "chan"),
            P(None, "chan"),
            P(None, "chan"),
            P(None, None, "chan", None),
            P(None, "chan"),
            P(None, "chan"),
            P(None, None, "chan"),
            P(None, "chan"),
        ),
        out_specs=P(("groups", "seq"), "chan"),
        check_vma=False,
    )
```

```python
import jax
import jax.numpy as jnp
from jax import lax
from jax.experimental import pallas as pl
from jax.experimental.pallas import tpu as pltpu
from jax.sharding import PartitionSpec as P


D0 = 32
D1 = 48
HALO = D0 + D1
EXTRA = 16
PIECE = 32
COST = {"k0": 100}
BF = jnp.bfloat16
F32 = jnp.float32
VM = pl.BlockSpec(memory_space=pltpu.VMEM)
HBM = pl.BlockSpec(memory_space=pltpu.HBM)
GRANT = 14 << 20


def call(name, kernel, outs, hbm, vmem, scratch=(), grant=GRANT):
    hbm = [pltpu.with_memory_space_constraint(a, pltpu.HBM) for a in hbm]
    vmem = [pltpu.with_memory_space_constraint(a, pltpu.VMEM) for a in vmem]
    return pl.pallas_call(
        kernel,
        out_shape=[pltpu.VMEM(shape, dtype) for shape, dtype in outs],
        in_specs=[HBM] * len(hbm) + [VM] * len(vmem),
        out_specs=[VM] * len(outs),
        scratch_shapes=list(scratch),
        compiler_params=pltpu.CompilerParams(vmem_limit_bytes=grant),
        cost_estimate=pl.CostEstimate(
            flops=COST.get(name, 3) * 10**9, bytes_accessed=0, transcendentals=0
        ),
    )(*hbm, *vmem)


def gelu(v):
    inner = v * (BF(0.7978845608028654) + BF(0.035677408136300125) * (v * v))
    half = BF(0.5) * v
    return half + half * jnp.tanh(inner)


def dot(a, b):
    return jnp.dot(a, b, preferred_element_type=F32)


def tiles(start, stop, step):
    return [(i, min(step, stop - i)) for i in range(start, stop, step)]


def act_rows(x, s_ref, b_ref, layer):
    return gelu(x * s_ref[layer : layer + 1].astype(BF) + b_ref[layer : layer + 1].astype(BF))


def taps(h_ref, base, spread, n):
    return jnp.concatenate(
        [h_ref[base + k * spread : base + k * spread + n] for k in (-1, 0, 1)], axis=1
    )


def put_mid(z_ref, own, other, mid_ref, layer, start, n):
    for i, m in tiles(start, start + n, PIECE):
        scale = mid_ref[layer : layer + 1].astype(BF)
        z_ref[i : i + m] = gelu(
            (own[i : i + m] + other[i : i + m]) * scale
            + mid_ref[2 + layer : 3 + layer].astype(BF)
        )


def sigmoid(v):
    return 0.5 + 0.5 * jnp.tanh(0.5 * v)


def embed_edges(rows):
    def kernel(
        tower, dna, embed, ins, inb, mids, midb,
        e_a, e_b, codes, embed_v, s_in, b_in, own_mid, dna_v, ends, mids_v, midb_v, sem,
    ):
        cp = pltpu.make_async_copy
        step = 128
        copies = [
            cp(dna, dna_v, sem.at[0]), cp(embed, embed_v, sem.at[1]),
            cp(tower.at[pl.ds(0, HALO)], ends.at[0], sem.at[2]),
            cp(tower.at[pl.ds(rows - HALO, HALO)], ends.at[1], sem.at[3]),
            cp(ins, s_in, sem.at[4]), cp(inb, b_in, sem.at[5]),
            cp(mids, mids_v, sem.at[6]), cp(midb, midb_v, sem.at[7]),
        ]
        for c in copies:
            c.start()
        slots = dna.shape[0]
        row = lax.broadcasted_iota(jnp.int32, (4 * slots, slots), 0)
        col = lax.broadcasted_iota(jnp.int32, (4 * slots, slots), 1)
        spread_map = jnp.where((row >> 2) == col, 1.0, 0.0).astype(BF)
        code = (lax.broadcasted_iota(jnp.int32, (4 * slots, step), 0) & 3).astype(F32)
        for c in copies:
            c.wait()
        for i, n in tiles(0, rows, step):
            base = dot(spread_map, dna_v[:, i : i + n].astype(F32).astype(BF))
            codes[i : i + n] = jnp.where(base == code, 1.0, 0.0).T.astype(BF)
        even = lax.rem(lax.axis_index("seq"), 2) == 0
        low = (ends[0].astype(F32) + dot(codes[0:HALO], embed_v[...])).astype(BF)
        high = (ends[1].astype(F32) + dot(codes[rows - HALO : rows], embed_v[...])).astype(BF)
        e_a[...] = jnp.where(even, high, low)
        e_b[...] = jnp.where(even, low, high)
        first = lax.axis_index("chan") == 0
        mid = jnp.concatenate([mids_v[...], midb_v[...]], axis=0)
        own_mid[...] = jnp.concatenate(
            [jnp.where(first, mid, 0.0), jnp.where(first, 0.0, mid)], axis=1
        )

    return kernel


def embed_first(a_lo, a_hi, rows):
    def kernel(tower, codes, embed, s_in, b_in, conv_w, own_mid, x0, h0, pa, emb):
        step = 128

        def embed_tile(i, n):
            emb[i : i + n] = dot(codes[i : i + n], embed[...])

        def act_tile(start, n):
            for i, m in tiles(start, start + n, PIECE):
                x = (tower[i : i + m].astype(F32) + emb[i : i + m]).astype(BF)
                x0[i : i + m] = x
                h0[i : i + m] = act_rows(x, s_in, b_in, 0)

        work = tiles(0, rows, step)
        embed_tile(*work[0])
        convs = tiles(a_lo, a_hi, step)
        for t in range(len(work)):
            if t + 1 < len(work):
                embed_tile(*work[t + 1])
            act_tile(*work[t])
            if convs and sum(convs[0]) + D0 <= t * step:
                i, n = convs.pop(0)
                pa[i - a_lo : i - a_lo + n] = dot(taps(h0, i, D0, n), conv_w[0]).astype(BF)
        assert not convs
        mid = own_mid[...]
        big = mid.astype(BF)
        rest = mid - big.astype(F32)
        middle = rest.astype(BF)
        small = (rest - middle.astype(F32)).astype(BF)
        pa[a_hi - a_lo : a_hi - a_lo + EXTRA] = jnp.concatenate(
            [big.astype(F32), middle.astype(F32), small.astype(F32), jnp.zeros_like(mid)], axis=0
        ).astype(BF)

    return kernel


def first_rest(b_lo, b_hi):
    def kernel(h0, conv_w, pb):
        pb[...] = dot(taps(h0, b_lo, D0, b_hi - b_lo), conv_w[0]).astype(BF)

    return kernel


def first_edges(rows):
    def kernel(r_a, r_b, h0, conv_w, s_in, b_in, pe, lo, hi, ext):
        seq = lax.axis_index("seq")
        even = lax.rem(seq, 2) == 0
        inner = 2 * D0
        span = HALO + inner
        ext[HALO:span] = h0[0:inner]
        ext[span : span + inner] = h0[rows - inner : rows]
        ends = (
            (lo, r_b, r_a, 0, seq == 0),
            (hi, r_a, r_b, span + inner, seq == lax.axis_size("seq") - 1),
        )
        for i, m in tiles(0, HALO, PIECE):
            zero = jnp.zeros((m, h0.shape[1]), BF)
            for keep, at_even, at_odd, at, outside in ends:
                x = jnp.where(even, at_even[i : i + m], at_odd[i : i + m])
                keep[i : i + m] = x
                ext[at + i : at + i + m] = jnp.where(outside, zero, act_rows(x, s_in, b_in, 0))
        lhs = [taps(ext, s + D0, D0, HALO) for s in (0, span)]
        pe[...] = dot(jnp.concatenate(lhs, axis=0), conv_w[0]).astype(BF)

    return kernel


def second_first(a_lo, a_hi, c_lo, c_hi):
    def kernel(
        pa, ra, x0, point_w, conv_w, s_in, b_in, own_mid, x1a, h1a, qa, mid, z, acc,
    ):
        step = 128
        n_a = a_hi - a_lo
        tail = ra[n_a : n_a + EXTRA].astype(F32)
        mid[...] = own_mid[...] + (tail[0:4] + tail[4:8] + tail[8:12])
        work = tiles(0, n_a, step)
        convs = tiles(c_lo, c_hi, step)

        def act_tile(start, n):
            for i, m in tiles(start, start + n, PIECE):
                x = (x0[a_lo + i : a_lo + i + m].astype(F32) + acc[i : i + m]).astype(BF)
                x1a[i : i + m] = x
                h1a[i : i + m] = act_rows(x, s_in, b_in, 1)

        put_mid(z, pa, ra, mid, 0, *work[0])
        for t in range(len(work) + 2 + len(convs)):
            if t + 1 < len(work):
                put_mid(z, pa, ra, mid, 0, *work[t + 1])
            if 1 <= t <= len(work):
                act_tile(*work[t - 1])
            if t < len(work):
                i, n = work[t]
                acc[i : i + n] = dot(z[i : i + n], point_w[0])
            if convs and sum(convs[0]) + D1 - a_lo <= (t - 1) * step:
                i, n = convs.pop(0)
                qa[i - c_lo : i - c_lo + n] = dot(taps(h1a, i - a_lo, D1, n), conv_w[1]).astype(BF)
        assert not convs

    return kernel


def second_rest(rows, a_lo, a_hi, c_hi, e_hi):
    def kernel(
        pb, rb, x0, x1a, h1a, point_w, conv_w, mid, s_in, b_in, x1b, x1t, h1t, qb, h1, z, acc
    ):
        step = 224
        b_hi = rows - D0
        first = c_hi - D1
        h1[0 : a_hi - first] = h1a[first - a_lo : a_hi - a_lo]
        x1b[0 : a_hi - c_hi] = x1a[c_hi - a_lo : a_hi - a_lo]
        work = tiles(0, b_hi - a_hi, step)
        convs = tiles(c_hi, e_hi, step)

        def act_tile(start, n):
            for i, m in tiles(start, start + n, PIECE):
                g = a_hi + i
                x = (x0[g : g + m].astype(F32) + acc[i : i + m]).astype(BF)
                h1[g - first : g - first + m] = act_rows(x, s_in, b_in, 1)
                keep = max(0, min(m, e_hi - g))
                if keep:
                    x1b[g - c_hi : g - c_hi + keep] = x[0:keep]
                if keep < m:
                    x1t[g + keep - e_hi : g + m - e_hi] = x[keep:]

        put_mid(z, pb, rb, mid, 0, *work[0])
        for t in range(len(work) + 2 + len(convs)):
            if t + 1 < len(work):
                put_mid(z, pb, rb, mid, 0, *work[t + 1])
            if 1 <= t <= len(work):
                act_tile(*work[t - 1])
            if t < len(work):
                i, n = work[t]
                acc[i : i + n] = dot(z[i : i + n], point_w[0])
            if t >= 2 and convs:
                i, n = convs.pop(0)
                qb[i - c_hi : i - c_hi + n] = dot(taps(h1, i - first, D1, n), conv_w[1]).astype(BF)
        h1t[...] = h1[e_hi - D1 - first : b_hi - first]

    return kernel


def second_edges(rows, a_lo, c_lo, e_hi):
    def kernel(
        pe, re, x0, lo, hi, x1a, h1a, x1t, h1t, point_w, conv_w, mid, s_in, b_in, x1c, qc, ext, z, acc
    ):
        seq = lax.axis_index("seq")
        tail = rows - D0 - e_hi
        top = c_lo + 2 * D1
        bottom = rows - e_hi + 2 * D1
        put_mid(z, pe, re, mid, 0, 0, 2 * HALO)
        acc[...] = dot(z[...], point_w[0])
        x1c[D0:c_lo] = x1a[0 : c_lo - a_lo]
        x1c[c_lo : c_lo + tail] = x1t[...]
        ext[HALO:top] = h1a[0 : c_lo + D1 - a_lo]
        ext[top : top + bottom - HALO] = h1t[...]
        low = top + bottom - HALO
        parts = (
            (0, 32, lo, HALO - D1, 0, None, seq == 0),
            (32, 16, lo, HALO - 16, 32, None, seq == 0),
            (D1, D0, x0, 0, D1, 0, None),
            (HALO, D0, x0, rows - D0, low, c_lo + tail, None),
            (HALO + D0, 32, hi, 0, low + D0, None, seq == lax.axis_size("seq") - 1),
            (HALO + D0 + 32, 16, hi, 32, low + D0 + 32, None, seq == lax.axis_size("seq") - 1),
        )
        for i, m, base, at, to, keep, outside in parts:
            x = (base[at : at + m].astype(F32) + acc[i : i + m]).astype(BF)
            h = act_rows(x, s_in, b_in, 1)
            if keep is not None:
                x1c[keep : keep + m] = x
            if outside is not None:
                h = jnp.where(outside, jnp.zeros_like(h), h)
            ext[to : to + m] = h
        lhs = [taps(ext, s + D1, D1, n) for s, n in ((0, c_lo), (top, rows - e_hi))]
        qc[...] = dot(jnp.concatenate(lhs, axis=0), conv_w[1]).astype(BF)

    return kernel


def own_half(width):
    chan = lax.axis_index("chan")
    mine = pl.ds(pl.multiple_of(chan * width, 128), width)
    theirs = pl.ds(pl.multiple_of((1 - chan) * width, 128), width)
    return mine, theirs


def last_point(x_base, n_rows, step, has_pool):
    def kernel(q, r, x1, point_w, mid, *rest):
        if has_pool:
            d_prev, pool, dm, xo, l_prev, z, acc, x2 = rest
        else:
            dm, xo, z, acc, x2 = rest
        half = step // 2
        row = lax.broadcasted_iota(jnp.int32, (step, step), 0)
        col = lax.broadcasted_iota(jnp.int32, (step, step), 1)
        pair = jnp.where(row < half, row, row - half) * 2
        pick = jnp.where(col == pair + 1, jnp.where(row < half, -1.0, 1.0), 0.0)
        pick = jnp.where((col == pair) & (row < half), 1.0, pick).astype(BF)

        def sum_rows(start, n):
            for i, m in tiles(start, start + n, PIECE):
                x = x1[x_base + i : x_base + i + m].astype(F32) + acc[i : i + m]
                x2[i : i + m] = x.astype(BF)

        def pair_rows(start, n):
            j = start // 2
            both = dot(pick, x2[start : start + n])
            dm[j : j + half] = both[:half].astype(BF)
            xo[j : j + half] = both[half:].astype(BF)

        work = tiles(0, n_rows, step)
        put_mid(z, q, r, mid, 1, *work[0])
        if has_pool:
            l_prev[...] = dot(d_prev[...], pool[own_half(x1.shape[1])[0], :])
        for t in range(len(work) + 2):
            if t + 1 < len(work):
                put_mid(z, q, r, mid, 1, *work[t + 1])
            if 1 <= t <= len(work):
                sum_rows(*work[t - 1])
            if t < len(work):
                i, n = work[t]
                acc[i : i + n] = dot(z[i : i + n], point_w[1])
            if t >= 2:
                pair_rows(*work[t - 2])

    return kernel


def finish(y, xo, d, logit):
    for i, m in tiles(0, y.shape[0], PIECE):
        y[i : i + m] = (
            xo[i : i + m].astype(F32) + sigmoid(logit[i : i + m]) * d[i : i + m].astype(F32)
        ).astype(BF)


def pool_first(ra, la, rb, lb, dc, pool, da, xoa, db, xob, ya, yb, lc, acc_a, acc_b):
    mine, theirs = own_half(ra.shape[1])
    acc_a[...] = la[...] + dot(ra[...], pool[theirs, :])
    acc_b[...] = lb[...] + dot(rb[...], pool[theirs, :])
    finish(ya, xoa, da, acc_a)
    lc[...] = dot(dc[...], pool[mine, :])
    finish(yb, xob, db, acc_b)


def pool_last(p_lo, p_hi, p_end):
    def kernel(rc, lc, pool, dc, xoc, ya, yb, out, y, acc, sem):
        theirs = own_half(rc.shape[1])[1]
        copy = pltpu.make_async_copy
        last = rc.shape[0] - p_lo
        copies = [
            copy(ya, out.at[pl.ds(p_lo, p_hi - p_lo)], sem.at[0]),
            copy(yb, out.at[pl.ds(p_hi, p_end - p_hi)], sem.at[1]),
            copy(y.at[pl.ds(0, p_lo)], out.at[pl.ds(0, p_lo)], sem.at[2]),
            copy(y.at[pl.ds(p_lo, last)], out.at[pl.ds(p_end, last)], sem.at[3]),
        ]
        copies[0].start()
        copies[1].start()
        acc[...] = lc[...] + dot(rc[...], pool[theirs, :])
        finish(y, xoc, dc, acc)
        copies[2].start()
        copies[3].start()
        for c in copies:
            c.wait()

    return kernel


def swap_chan(a):
    return lax.ppermute(a, "chan", [(0, 1), (1, 0)])


def local(
    tower_input, dna_bases, base_embed, in_scale, entry_norm_shift,
    conv_w, mid_scale, mid_shift, point_w, pooling_weight,
):
    rows, width = tower_input.shape
    inner = conv_w.shape[3]
    a_lo, a_hi = D0, rows // 2 + 32
    c_lo, c_hi, e_hi = 96, rows // 2 - 32, rows - 96
    b_hi = rows - D0
    n_a, n_b = a_hi - a_lo, b_hi - a_hi
    m_a, m_b = c_hi - c_lo, e_hi - c_hi
    m_c = rows - m_a - m_b
    dma = pltpu.SemaphoreType.DMA
    weights = conv_w.reshape(conv_w.shape[0], 3 * width, inner)
    e_a, e_b, codes, embed, s_in, b_in, own_mid = call(
        "k0",
        embed_edges(rows),
        [
            ((HALO, width), BF), ((HALO, width), BF), ((rows, base_embed.shape[0]), BF),
            (base_embed.shape, BF), ((2, width), F32), ((2, width), F32), ((4, inner), F32),
        ],
        [
            tower_input, dna_bases.T, base_embed, in_scale, entry_norm_shift, mid_scale, mid_shift,
        ],
        [],
        [
            pltpu.VMEM(dna_bases.shape[::-1], jnp.int32), pltpu.VMEM((2, HALO, width), BF),
            pltpu.VMEM(mid_scale.shape, F32), pltpu.VMEM(mid_shift.shape, F32), dma((8,)),
        ],
    )
    x0, h0, pa = call(
        "k1a",
        embed_first(a_lo, a_hi, rows),
        [((rows, width), BF), ((rows, width), BF), ((n_a + EXTRA, inner), BF)],
        [],
        [tower_input, codes, embed, s_in, b_in, weights, own_mid],
        [pltpu.VMEM((rows, width), F32)],
    )
    ra = swap_chan(pa)
    count = lax.axis_size("seq")
    pairs_a = [(i, i ^ 1) for i in range(count)]
    pairs_b = [(i, ((i - 1) ^ 1) + 1) for i in range(1, count - 1)]
    r_a = lax.ppermute(e_a, "seq", pairs_a)
    r_b = lax.ppermute(e_b, "seq", pairs_b)
    (pb,) = call("k1b", first_rest(a_hi, b_hi), [((n_b, inner), BF)], [], [h0, weights])
    rb = swap_chan(pb)
    x1a, h1a, qa, mid = call(
        "k2a",
        second_first(a_lo, a_hi, c_lo, c_hi),
        [
            ((n_a, width), BF), ((n_a, width), BF), ((m_a, inner), BF), ((4, inner), F32),
        ],
        [],
        [pa, ra, x0, point_w, weights, s_in, b_in, own_mid],
        [pltpu.VMEM((n_a, inner), BF), pltpu.VMEM((n_a, width), F32)],
    )
    sa = swap_chan(qa)
    pe, lo, hi = call(
        "k1e",
        first_edges(rows),
        [((2 * HALO, inner), BF), ((HALO, width), BF), ((HALO, width), BF)],
        [],
        [r_a, r_b, h0, weights, s_in, b_in],
        [pltpu.VMEM((2 * (HALO + 2 * D0), width), BF)],
    )
    re = swap_chan(pe)
    x1b, x1t, h1t, qb = call(
        "k2b",
        second_rest(rows, a_lo, a_hi, c_hi, e_hi),
        [
            ((m_b, width), BF), ((b_hi - e_hi, width), BF),
            ((b_hi - e_hi + D1, width), BF), ((m_b, inner), BF),
        ],
        [],
        [pb, rb, x0, x1a, h1a, point_w, weights, mid, s_in, b_in],
        [
            pltpu.VMEM((b_hi - c_hi + D1, width), BF), pltpu.VMEM((n_b, inner), BF),
            pltpu.VMEM((n_b, width), F32),
        ],
    )
    sb = swap_chan(qb)
    x1c, qc = call(
        "k2c",
        second_edges(rows, a_lo, c_lo, e_hi),
        [((m_c, width), BF), ((m_c, inner), BF)],
        [],
        [pe, re, x0, lo, hi, x1a, h1a, x1t, h1t, point_w, weights, mid, s_in, b_in],
        [
            pltpu.VMEM((m_c + 4 * D1, width), BF), pltpu.VMEM((2 * HALO, inner), BF),
            pltpu.VMEM((2 * HALO, width), F32),
        ],
    )
    sc = swap_chan(qc)
    ends, halves = [], []
    for name, q, s, x1, base, m, step in (
        ("a", qa, sa, x1a, c_lo - a_lo, m_a, 128),
        ("b", qb, sb, x1b, 0, m_b, 224),
        ("c", qc, sc, x1c, 0, m_c, 192),
    ):
        before = [ends[-1][0], pooling_weight] if ends else []
        dm, xo, *half = call(
            "k3" + name,
            last_point(base, m, step, bool(before)),
            [((m // 2, width), BF), ((m // 2, width), BF)]
            + [((d.shape[0], width), F32) for d in before[:1]],
            [],
            [q, s, x1, point_w, mid, *before],
            [
                pltpu.VMEM((m, inner), BF), pltpu.VMEM((m, width), F32),
                pltpu.VMEM((m, width), BF),
            ],
        )
        halves += half
        ends.append((dm, swap_chan(dm), xo))
    (da, ta, xoa), (db, tb, xob), (dc, tc, xoc) = ends
    la, lb = halves
    ya, yb, lc = call(
        "k4",
        pool_first,
        [((m_a // 2, width), BF), ((m_b // 2, width), BF), ((m_c // 2, width), F32)],
        [],
        [ta, la, tb, lb, dc, pooling_weight, da, xoa, db, xob],
        [pltpu.VMEM((m_a // 2, width), F32), pltpu.VMEM((m_b // 2, width), F32)],
    )
    vm = [
        pltpu.with_memory_space_constraint(a, pltpu.VMEM)
        for a in (tc, lc, pooling_weight, dc, xoc, ya, yb)
    ]
    return pl.pallas_call(
        pool_last(c_lo // 2, c_hi // 2, e_hi // 2),
        out_shape=jax.ShapeDtypeStruct((rows // 2, width), BF),
        in_specs=[VM] * 7,
        out_specs=HBM,
        scratch_shapes=[
            pltpu.VMEM((m_c // 2, width), BF), pltpu.VMEM((m_c // 2, width), F32), dma((4,)),
        ],
        compiler_params=pltpu.CompilerParams(vmem_limit_bytes=GRANT),
    )(*vm)


def solution(mesh):
    return jax.shard_map(
        local,
        mesh=mesh,
        in_specs=(
            P(("groups", "seq"), "chan"),
            P(("groups", "seq"), None),
            P(None, "chan"),
            P(None, "chan"),
            P(None, "chan"),
            P(None, None, "chan", None),
            P(None, "chan"),
            P(None, "chan"),
            P(None, None, "chan"),
            P(None, "chan"),
        ),
        out_specs=P(("groups", "seq"), "chan"),
        check_vma=False,
    )
```

```python
import jax
import jax.numpy as jnp
from jax import lax
from jax.experimental import pallas as pl
from jax.experimental.pallas import tpu as pltpu
from jax.sharding import PartitionSpec as P


D0 = 32
D1 = 48
HALO = D0 + D1
EXTRA = 16
PIECE = 32
COST = {"k0": 100}
BF = jnp.bfloat16
F32 = jnp.float32
VM = pl.BlockSpec(memory_space=pltpu.VMEM)
HBM = pl.BlockSpec(memory_space=pltpu.HBM)
GRANT = 14 << 20


def call(name, kernel, outs, hbm, vmem, scratch=(), grant=GRANT):
    hbm = [pltpu.with_memory_space_constraint(a, pltpu.HBM) for a in hbm]
    vmem = [pltpu.with_memory_space_constraint(a, pltpu.VMEM) for a in vmem]
    return pl.pallas_call(
        kernel,
        out_shape=[pltpu.VMEM(shape, dtype) for shape, dtype in outs],
        in_specs=[HBM] * len(hbm) + [VM] * len(vmem),
        out_specs=[VM] * len(outs),
        scratch_shapes=list(scratch),
        compiler_params=pltpu.CompilerParams(vmem_limit_bytes=grant),
        cost_estimate=pl.CostEstimate(
            flops=COST.get(name, 3) * 10**9, bytes_accessed=0, transcendentals=0
        ),
    )(*hbm, *vmem)


def gelu(v):
    inner = v * (BF(0.7978845608028654) + BF(0.035677408136300125) * (v * v))
    half = BF(0.5) * v
    return half + half * jnp.tanh(inner)


def dot(a, b):
    return jnp.dot(a, b, preferred_element_type=F32)


def tiles(start, stop, step):
    return [(i, min(step, stop - i)) for i in range(start, stop, step)]


def act_rows(x, s_ref, b_ref, layer):
    return gelu(x * s_ref[layer : layer + 1].astype(BF) + b_ref[layer : layer + 1].astype(BF))


def taps(h_ref, base, spread, n):
    return jnp.concatenate(
        [h_ref[base + k * spread : base + k * spread + n] for k in (-1, 0, 1)], axis=1
    )


def put_weights(dst, conv_w, layer, start, stop):
    width = dst.shape[1]
    half = BF(0.5)
    for i, m in tiles(start, stop, PIECE):
        outer = conv_w[layer, i : i + m] + conv_w[layer, 2 * width + i : 2 * width + i + m]
        outer = half * outer
        inner = half * conv_w[layer, width + i : width + i + m]
        dst[0, i : i + m] = outer + inner
        dst[1, i : i + m] = outer - inner


def pair_conv(h_ref, base, spread, n, conv_w, layer, both, dst, v, between=()):
    width = both.shape[1]
    between = list(between)
    for t in range(n // (2 * spread)):
        s = base + 2 * spread * t
        x0, x1, x2, x3 = (h_ref[s + k * spread : s + (k + 1) * spread] for k in (-1, 0, 1, 2))
        rows = slice(t * spread, (t + 1) * spread)
        v[0, rows] = x0 - x2
        v[1, rows] = x1 + x2
        v[2, rows] = x2 - x1
        v[3, rows] = x1 - x3
    cols = dst.shape[1]
    for c in range(0, cols, 256):
        if between:
            between.pop(0)()
        q = slice(c, min(c + 256, cols))
        m1 = dot(v[0], conv_w[layer, 0:width, q])
        m2 = dot(v[1], both[0, :, q])
        m3 = dot(v[2], both[1, :, q])
        m4 = dot(v[3], conv_w[layer, 2 * width : 3 * width, q])
        y0 = (m1 + (m2 + m3)).astype(BF)
        y1 = ((m2 - m3) - m4).astype(BF)
        for t in range(n // (2 * spread)):
            rows = slice(t * spread, (t + 1) * spread)
            at = 2 * spread * t
            dst[at : at + spread, q] = y0[rows]
            dst[at + spread : at + 2 * spread, q] = y1[rows]


def put_mid(z_ref, own, other, mid_ref, layer, start, n):
    for i, m in tiles(start, start + n, PIECE):
        scale = mid_ref[layer : layer + 1].astype(BF)
        z_ref[i : i + m] = gelu(
            (own[i : i + m] + other[i : i + m]) * scale
            + mid_ref[2 + layer : 3 + layer].astype(BF)
        )


def sigmoid(v):
    return 0.5 + 0.5 * jnp.tanh(0.5 * v)


def embed_edges(rows):
    def kernel(
        tower, dna, embed, ins, inb, mids, midb,
        e_a, e_b, codes, embed_v, s_in, b_in, own_mid, dna_v, ends, mids_v, midb_v, sem,
    ):
        cp = pltpu.make_async_copy
        step = 128
        copies = [
            cp(dna, dna_v, sem.at[0]), cp(embed, embed_v, sem.at[1]),
            cp(tower.at[pl.ds(0, HALO)], ends.at[0], sem.at[2]),
            cp(tower.at[pl.ds(rows - HALO, HALO)], ends.at[1], sem.at[3]),
            cp(ins, s_in, sem.at[4]), cp(inb, b_in, sem.at[5]),
            cp(mids, mids_v, sem.at[6]), cp(midb, midb_v, sem.at[7]),
        ]
        for c in copies:
            c.start()
        slots = dna.shape[0]
        row = lax.broadcasted_iota(jnp.int32, (4 * slots, slots), 0)
        col = lax.broadcasted_iota(jnp.int32, (4 * slots, slots), 1)
        spread_map = jnp.where((row >> 2) == col, 1.0, 0.0).astype(BF)
        code = (lax.broadcasted_iota(jnp.int32, (4 * slots, step), 0) & 3).astype(F32)
        for c in copies:
            c.wait()
        for i, n in tiles(0, rows, step):
            base = dot(spread_map, dna_v[:, i : i + n].astype(F32).astype(BF))
            codes[i : i + n] = jnp.where(base == code, 1.0, 0.0).T.astype(BF)
        even = lax.rem(lax.axis_index("seq"), 2) == 0
        low = (ends[0].astype(F32) + dot(codes[0:HALO], embed_v[...])).astype(BF)
        high = (ends[1].astype(F32) + dot(codes[rows - HALO : rows], embed_v[...])).astype(BF)
        e_a[...] = jnp.where(even, high, low)
        e_b[...] = jnp.where(even, low, high)
        first = lax.axis_index("chan") == 0
        mid = jnp.concatenate([mids_v[...], midb_v[...]], axis=0)
        own_mid[...] = jnp.concatenate(
            [jnp.where(first, mid, 0.0), jnp.where(first, 0.0, mid)], axis=1
        )

    return kernel


def embed_first(a_lo, a_hi, rows):
    def kernel(tower, codes, embed, s_in, b_in, conv_w, own_mid, x0, h0, pa, both, emb, v):
        step = 128

        def embed_tile(i, n):
            emb[i : i + n] = dot(codes[i : i + n], embed[...])

        def act_tile(start, n):
            for i, m in tiles(start, start + n, PIECE):
                x = (tower[i : i + m].astype(F32) + emb[i : i + m]).astype(BF)
                x0[i : i + m] = x
                h0[i : i + m] = act_rows(x, s_in, b_in, 0)

        work = tiles(0, rows, step)
        embed_tile(*work[0])

        def stage(t):
            if t + 1 < len(work):
                embed_tile(*work[t + 1])
            act_tile(*work[t])

        need = -(-(a_hi + D0) // step)
        for t in range(need):
            stage(t)
        put_weights(both, conv_w, 0, 0, both.shape[1])
        later = [lambda t=t: stage(t) for t in range(need, len(work))]
        pair_conv(h0, a_lo, D0, a_hi - a_lo, conv_w, 0, both, pa, v, later[:3])
        for f in later[3:]:
            f()
        mid = own_mid[...]
        big = mid.astype(BF)
        rest = mid - big.astype(F32)
        middle = rest.astype(BF)
        small = (rest - middle.astype(F32)).astype(BF)
        pa[a_hi - a_lo : a_hi - a_lo + EXTRA] = jnp.concatenate(
            [big.astype(F32), middle.astype(F32), small.astype(F32), jnp.zeros_like(mid)], axis=0
        ).astype(BF)

    return kernel


def first_rest(b_lo, b_hi):
    def kernel(h0, conv_w, both, pb, both_next, v):
        third = both.shape[1] // 3
        later = [
            lambda k=k: put_weights(both_next, conv_w, 1, k * third, (k + 1) * third)
            for k in range(3)
        ]
        pair_conv(h0, b_lo, D0, b_hi - b_lo, conv_w, 0, both, pb, v, later)

    return kernel


def first_edges(rows):
    def kernel(r_a, r_b, h0, conv_w, s_in, b_in, pe, lo, hi, ext):
        seq = lax.axis_index("seq")
        even = lax.rem(seq, 2) == 0
        inner = 2 * D0
        span = HALO + inner
        ext[HALO:span] = h0[0:inner]
        ext[span : span + inner] = h0[rows - inner : rows]
        ends = (
            (lo, r_b, r_a, 0, seq == 0),
            (hi, r_a, r_b, span + inner, seq == lax.axis_size("seq") - 1),
        )
        for i, m in tiles(0, HALO, PIECE):
            zero = jnp.zeros((m, h0.shape[1]), BF)
            for keep, at_even, at_odd, at, outside in ends:
                x = jnp.where(even, at_even[i : i + m], at_odd[i : i + m])
                keep[i : i + m] = x
                ext[at + i : at + i + m] = jnp.where(outside, zero, act_rows(x, s_in, b_in, 0))
        lhs = [taps(ext, s + D0, D0, HALO) for s in (0, span)]
        pe[...] = dot(jnp.concatenate(lhs, axis=0), conv_w[0]).astype(BF)

    return kernel


def second_first(a_lo, a_hi, c_lo, c_hi):
    def kernel(
        pa, ra, x0, point_w, conv_w, both, s_in, b_in, own_mid, x1a, h1a, qa, mid, z, acc, v,
    ):
        step = 128
        n_a = a_hi - a_lo
        tail = ra[n_a : n_a + EXTRA].astype(F32)
        mid[...] = own_mid[...] + (tail[0:4] + tail[4:8] + tail[8:12])
        work = tiles(0, n_a, step)

        def act_tile(start, n):
            for i, m in tiles(start, start + n, PIECE):
                x = (x0[a_lo + i : a_lo + i + m].astype(F32) + acc[i : i + m]).astype(BF)
                x1a[i : i + m] = x
                h1a[i : i + m] = act_rows(x, s_in, b_in, 1)

        put_mid(z, pa, ra, mid, 0, *work[0])
        for t in range(len(work) + 1):
            if t + 1 < len(work):
                put_mid(z, pa, ra, mid, 0, *work[t + 1])
            if 1 <= t <= len(work):
                act_tile(*work[t - 1])
            if t < len(work):
                i, n = work[t]
                acc[i : i + n] = dot(z[i : i + n], point_w[0])
        pair_conv(h1a, c_lo - a_lo, D1, c_hi - c_lo, conv_w, 1, both, qa, v)

    return kernel


def second_rest(rows, a_lo, a_hi, c_hi, e_hi):
    def kernel(
        pb, rb, x0, x1a, h1a, point_w, conv_w, both, mid, s_in, b_in, x1b, x1t, h1t, qb, h1, z, acc, v
    ):
        step = 224
        b_hi = rows - D0
        first = c_hi - D1
        h1[0 : a_hi - first] = h1a[first - a_lo : a_hi - a_lo]
        x1b[0 : a_hi - c_hi] = x1a[c_hi - a_lo : a_hi - a_lo]
        work = tiles(0, b_hi - a_hi, step)

        def act_tile(start, n):
            for i, m in tiles(start, start + n, PIECE):
                g = a_hi + i
                x = (x0[g : g + m].astype(F32) + acc[i : i + m]).astype(BF)
                h1[g - first : g - first + m] = act_rows(x, s_in, b_in, 1)
                keep = max(0, min(m, e_hi - g))
                if keep:
                    x1b[g - c_hi : g - c_hi + keep] = x[0:keep]
                if keep < m:
                    x1t[g + keep - e_hi : g + m - e_hi] = x[keep:]

        put_mid(z, pb, rb, mid, 0, *work[0])
        for t in range(len(work) + 1):
            if t + 1 < len(work):
                put_mid(z, pb, rb, mid, 0, *work[t + 1])
            if 1 <= t <= len(work):
                act_tile(*work[t - 1])
            if t < len(work):
                i, n = work[t]
                acc[i : i + n] = dot(z[i : i + n], point_w[0])
        pair_conv(h1, c_hi - first, D1, e_hi - c_hi, conv_w, 1, both, qb, v)
        h1t[...] = h1[e_hi - D1 - first : b_hi - first]

    return kernel


def second_edges(rows, a_lo, c_lo, e_hi):
    def kernel(
        pe, re, x0, lo, hi, x1a, h1a, x1t, h1t, point_w, conv_w, mid, s_in, b_in, x1c, qc, ext, z, acc
    ):
        seq = lax.axis_index("seq")
        tail = rows - D0 - e_hi
        top = c_lo + 2 * D1
        bottom = rows - e_hi + 2 * D1
        put_mid(z, pe, re, mid, 0, 0, 2 * HALO)
        acc[...] = dot(z[...], point_w[0])
        x1c[D0:c_lo] = x1a[0 : c_lo - a_lo]
        x1c[c_lo : c_lo + tail] = x1t[...]
        ext[HALO:top] = h1a[0 : c_lo + D1 - a_lo]
        ext[top : top + bottom - HALO] = h1t[...]
        low = top + bottom - HALO
        parts = (
            (0, 32, lo, HALO - D1, 0, None, seq == 0),
            (32, 16, lo, HALO - 16, 32, None, seq == 0),
            (D1, D0, x0, 0, D1, 0, None),
            (HALO, D0, x0, rows - D0, low, c_lo + tail, None),
            (HALO + D0, 32, hi, 0, low + D0, None, seq == lax.axis_size("seq") - 1),
            (HALO + D0 + 32, 16, hi, 32, low + D0 + 32, None, seq == lax.axis_size("seq") - 1),
        )
        for i, m, base, at, to, keep, outside in parts:
            x = (base[at : at + m].astype(F32) + acc[i : i + m]).astype(BF)
            h = act_rows(x, s_in, b_in, 1)
            if keep is not None:
                x1c[keep : keep + m] = x
            if outside is not None:
                h = jnp.where(outside, jnp.zeros_like(h), h)
            ext[to : to + m] = h
        lhs = [taps(ext, s + D1, D1, n) for s, n in ((0, c_lo), (top, rows - e_hi))]
        qc[...] = dot(jnp.concatenate(lhs, axis=0), conv_w[1]).astype(BF)

    return kernel


def own_half(width):
    chan = lax.axis_index("chan")
    mine = pl.ds(pl.multiple_of(chan * width, 128), width)
    theirs = pl.ds(pl.multiple_of((1 - chan) * width, 128), width)
    return mine, theirs


def last_point(x_base, n_rows, step, has_pool):
    def kernel(q, r, x1, point_w, mid, *rest):
        if has_pool:
            d_prev, pool, dm, xo, l_prev, z, acc, x2 = rest
        else:
            dm, xo, z, acc, x2 = rest
        half = step // 2
        row = lax.broadcasted_iota(jnp.int32, (step, step), 0)
        col = lax.broadcasted_iota(jnp.int32, (step, step), 1)
        pair = jnp.where(row < half, row, row - half) * 2
        pick = jnp.where(col == pair + 1, jnp.where(row < half, -1.0, 1.0), 0.0)
        pick = jnp.where((col == pair) & (row < half), 1.0, pick).astype(BF)

        def sum_rows(start, n):
            for i, m in tiles(start, start + n, PIECE):
                x = x1[x_base + i : x_base + i + m].astype(F32) + acc[i : i + m]
                x2[i : i + m] = x.astype(BF)

        def pair_rows(start, n):
            j = start // 2
            both = dot(pick, x2[start : start + n])
            dm[j : j + half] = both[:half].astype(BF)
            xo[j : j + half] = both[half:].astype(BF)

        work = tiles(0, n_rows, step)
        put_mid(z, q, r, mid, 1, *work[0])
        if has_pool:
            l_prev[...] = dot(d_prev[...], pool[own_half(x1.shape[1])[0], :])
        for t in range(len(work) + 2):
            if t + 1 < len(work):
                put_mid(z, q, r, mid, 1, *work[t + 1])
            if 1 <= t <= len(work):
                sum_rows(*work[t - 1])
            if t < len(work):
                i, n = work[t]
                acc[i : i + n] = dot(z[i : i + n], point_w[1])
            if t >= 2:
                pair_rows(*work[t - 2])

    return kernel


def finish(y, xo, d, logit):
    for i, m in tiles(0, y.shape[0], PIECE):
        y[i : i + m] = (
            xo[i : i + m].astype(F32) + sigmoid(logit[i : i + m]) * d[i : i + m].astype(F32)
        ).astype(BF)


def pool_first(ra, la, rb, lb, dc, pool, da, xoa, db, xob, ya, yb, lc, acc_a, acc_b):
    mine, theirs = own_half(ra.shape[1])
    acc_a[...] = la[...] + dot(ra[...], pool[theirs, :])
    acc_b[...] = lb[...] + dot(rb[...], pool[theirs, :])
    finish(ya, xoa, da, acc_a)
    lc[...] = dot(dc[...], pool[mine, :])
    finish(yb, xob, db, acc_b)


def pool_last(p_lo, p_hi, p_end):
    def kernel(rc, lc, pool, dc, xoc, ya, yb, out, y, acc, sem):
        theirs = own_half(rc.shape[1])[1]
        copy = pltpu.make_async_copy
        last = rc.shape[0] - p_lo
        copies = [
            copy(ya, out.at[pl.ds(p_lo, p_hi - p_lo)], sem.at[0]),
            copy(yb, out.at[pl.ds(p_hi, p_end - p_hi)], sem.at[1]),
            copy(y.at[pl.ds(0, p_lo)], out.at[pl.ds(0, p_lo)], sem.at[2]),
            copy(y.at[pl.ds(p_lo, last)], out.at[pl.ds(p_end, last)], sem.at[3]),
        ]
        copies[0].start()
        copies[1].start()
        acc[...] = lc[...] + dot(rc[...], pool[theirs, :])
        finish(y, xoc, dc, acc)
        copies[2].start()
        copies[3].start()
        for c in copies:
            c.wait()

    return kernel


def swap_chan(a):
    return lax.ppermute(a, "chan", [(0, 1), (1, 0)])


def local(
    tower_input, dna_bases, base_embed, in_scale, entry_norm_shift,
    conv_w, mid_scale, mid_shift, point_w, pooling_weight,
):
    rows, width = tower_input.shape
    inner = conv_w.shape[3]
    a_lo, a_hi = D0, rows // 2 + 32
    c_lo, c_hi, e_hi = 96, rows // 2 - 32, rows - 160
    b_hi = rows - D0
    n_a, n_b = a_hi - a_lo, b_hi - a_hi
    m_a, m_b = c_hi - c_lo, e_hi - c_hi
    m_c = rows - m_a - m_b
    dma = pltpu.SemaphoreType.DMA
    weights = conv_w.reshape(conv_w.shape[0], 3 * width, inner)
    e_a, e_b, codes, embed, s_in, b_in, own_mid = call(
        "k0",
        embed_edges(rows),
        [
            ((HALO, width), BF), ((HALO, width), BF), ((rows, base_embed.shape[0]), BF),
            (base_embed.shape, BF), ((2, width), F32), ((2, width), F32), ((4, inner), F32),
        ],
        [
            tower_input, dna_bases.T, base_embed, in_scale, entry_norm_shift, mid_scale, mid_shift,
        ],
        [],
        [
            pltpu.VMEM(dna_bases.shape[::-1], jnp.int32), pltpu.VMEM((2, HALO, width), BF),
            pltpu.VMEM(mid_scale.shape, F32), pltpu.VMEM(mid_shift.shape, F32), dma((8,)),
        ],
    )
    x0, h0, pa, both0 = call(
        "k1a",
        embed_first(a_lo, a_hi, rows),
        [
            ((rows, width), BF), ((rows, width), BF), ((n_a + EXTRA, inner), BF),
            ((2, width, inner), BF),
        ],
        [],
        [tower_input, codes, embed, s_in, b_in, weights, own_mid],
        [pltpu.VMEM((rows, width), F32), pltpu.VMEM((4, n_a // 2, width), BF)],
    )
    ra = swap_chan(pa)
    count = lax.axis_size("seq")
    pairs_a = [(i, i ^ 1) for i in range(count)]
    pairs_b = [(i, ((i - 1) ^ 1) + 1) for i in range(1, count - 1)]
    r_a = lax.ppermute(e_a, "seq", pairs_a)
    r_b = lax.ppermute(e_b, "seq", pairs_b)
    pb, both1 = call(
        "k1b",
        first_rest(a_hi, b_hi),
        [((n_b, inner), BF), ((2, width, inner), BF)],
        [],
        [h0, weights, both0],
        [pltpu.VMEM((4, n_b // 2, width), BF)],
    )
    rb = swap_chan(pb)
    x1a, h1a, qa, mid = call(
        "k2a",
        second_first(a_lo, a_hi, c_lo, c_hi),
        [
            ((n_a, width), BF), ((n_a, width), BF), ((m_a, inner), BF), ((4, inner), F32),
        ],
        [],
        [pa, ra, x0, point_w, weights, both1, s_in, b_in, own_mid],
        [
            pltpu.VMEM((n_a, inner), BF), pltpu.VMEM((n_a, width), F32),
            pltpu.VMEM((4, m_a // 2, width), BF),
        ],
    )
    sa = swap_chan(qa)
    pe, lo, hi = call(
        "k1e",
        first_edges(rows),
        [((2 * HALO, inner), BF), ((HALO, width), BF), ((HALO, width), BF)],
        [],
        [r_a, r_b, h0, weights, s_in, b_in],
        [pltpu.VMEM((2 * (HALO + 2 * D0), width), BF)],
    )
    re = swap_chan(pe)
    x1b, x1t, h1t, qb = call(
        "k2b",
        second_rest(rows, a_lo, a_hi, c_hi, e_hi),
        [
            ((m_b, width), BF), ((b_hi - e_hi, width), BF),
            ((b_hi - e_hi + D1, width), BF), ((m_b, inner), BF),
        ],
        [],
        [pb, rb, x0, x1a, h1a, point_w, weights, both1, mid, s_in, b_in],
        [
            pltpu.VMEM((b_hi - c_hi + D1, width), BF), pltpu.VMEM((n_b, inner), BF),
            pltpu.VMEM((n_b, width), F32), pltpu.VMEM((4, m_b // 2, width), BF),
        ],
    )
    sb = swap_chan(qb)
    x1c, qc = call(
        "k2c",
        second_edges(rows, a_lo, c_lo, e_hi),
        [((m_c, width), BF), ((m_c, inner), BF)],
        [],
        [pe, re, x0, lo, hi, x1a, h1a, x1t, h1t, point_w, weights, mid, s_in, b_in],
        [
            pltpu.VMEM((m_c + 4 * D1, width), BF), pltpu.VMEM((2 * HALO, inner), BF),
            pltpu.VMEM((2 * HALO, width), F32),
        ],
    )
    sc = swap_chan(qc)
    ends, halves = [], []
    for name, q, s, x1, base, m, step in (
        ("a", qa, sa, x1a, c_lo - a_lo, m_a, 128),
        ("b", qb, sb, x1b, 0, m_b, 128),
        ("c", qc, sc, x1c, 0, m_c, 128),
    ):
        before = [ends[-1][0], pooling_weight] if ends else []
        dm, xo, *half = call(
            "k3" + name,
            last_point(base, m, step, bool(before)),
            [((m // 2, width), BF), ((m // 2, width), BF)]
            + [((d.shape[0], width), F32) for d in before[:1]],
            [],
            [q, s, x1, point_w, mid, *before],
            [
                pltpu.VMEM((m, inner), BF), pltpu.VMEM((m, width), F32),
                pltpu.VMEM((m, width), BF),
            ],
        )
        halves += half
        ends.append((dm, swap_chan(dm), xo))
    (da, ta, xoa), (db, tb, xob), (dc, tc, xoc) = ends
    la, lb = halves
    ya, yb, lc = call(
        "k4",
        pool_first,
        [((m_a // 2, width), BF), ((m_b // 2, width), BF), ((m_c // 2, width), F32)],
        [],
        [ta, la, tb, lb, dc, pooling_weight, da, xoa, db, xob],
        [pltpu.VMEM((m_a // 2, width), F32), pltpu.VMEM((m_b // 2, width), F32)],
    )
    vm = [
        pltpu.with_memory_space_constraint(a, pltpu.VMEM)
        for a in (tc, lc, pooling_weight, dc, xoc, ya, yb)
    ]
    return pl.pallas_call(
        pool_last(c_lo // 2, c_hi // 2, e_hi // 2),
        out_shape=jax.ShapeDtypeStruct((rows // 2, width), BF),
        in_specs=[VM] * 7,
        out_specs=HBM,
        scratch_shapes=[
            pltpu.VMEM((m_c // 2, width), BF), pltpu.VMEM((m_c // 2, width), F32), dma((4,)),
        ],
        compiler_params=pltpu.CompilerParams(vmem_limit_bytes=GRANT),
    )(*vm)


def solution(mesh):
    return jax.shard_map(
        local,
        mesh=mesh,
        in_specs=(
            P(("groups", "seq"), "chan"),
            P(("groups", "seq"), None),
            P(None, "chan"),
            P(None, "chan"),
            P(None, "chan"),
            P(None, None, "chan", None),
            P(None, "chan"),
            P(None, "chan"),
            P(None, None, "chan"),
            P(None, "chan"),
        ),
        out_specs=P(("groups", "seq"), "chan"),
        check_vma=False,
    )
```

```python
import jax
import jax.numpy as jnp
from jax import lax
from jax.experimental import pallas as pl
from jax.experimental.pallas import tpu as pltpu
from jax.sharding import PartitionSpec as P


D0 = 32
D1 = 48
HALO = D0 + D1
EXTRA = 16
PIECE = 32
COST = {"k0": 100}
BF = jnp.bfloat16
F32 = jnp.float32
VM = pl.BlockSpec(memory_space=pltpu.VMEM)
HBM = pl.BlockSpec(memory_space=pltpu.HBM)
GRANT = 14 << 20


def call(name, kernel, outs, hbm, vmem, scratch=(), grant=GRANT):
    hbm = [pltpu.with_memory_space_constraint(a, pltpu.HBM) for a in hbm]
    vmem = [pltpu.with_memory_space_constraint(a, pltpu.VMEM) for a in vmem]
    return pl.pallas_call(
        kernel,
        out_shape=[pltpu.VMEM(shape, dtype) for shape, dtype in outs],
        in_specs=[HBM] * len(hbm) + [VM] * len(vmem),
        out_specs=[VM] * len(outs),
        scratch_shapes=list(scratch),
        compiler_params=pltpu.CompilerParams(vmem_limit_bytes=grant),
        cost_estimate=pl.CostEstimate(
            flops=COST.get(name, 3) * 10**9, bytes_accessed=0, transcendentals=0
        ),
    )(*hbm, *vmem)


def gelu(v):
    inner = v * (BF(0.7978845608028654) + BF(0.035677408136300125) * (v * v))
    half = BF(0.5) * v
    return half + half * jnp.tanh(inner)


def dot(a, b):
    return jnp.dot(a, b, preferred_element_type=F32)


def tiles(start, stop, step):
    return [(i, min(step, stop - i)) for i in range(start, stop, step)]


def act_rows(x, s_ref, b_ref, layer):
    return gelu(x * s_ref[layer : layer + 1].astype(BF) + b_ref[layer : layer + 1].astype(BF))


def taps(h_ref, base, spread, n):
    return jnp.concatenate(
        [h_ref[base + k * spread : base + k * spread + n] for k in (-1, 0, 1)], axis=1
    )


def put_weights(dst, conv_w, layer, start, stop):
    width = dst.shape[1]
    half = BF(0.5)
    for i, m in tiles(start, stop, PIECE):
        outer = conv_w[layer, i : i + m] + conv_w[layer, 2 * width + i : 2 * width + i + m]
        outer = half * outer
        inner = half * conv_w[layer, width + i : width + i + m]
        dst[0, i : i + m] = outer + inner
        dst[1, i : i + m] = outer - inner


def pair_conv(h_ref, base, spread, n, conv_w, layer, both, dst, v, between=(), early=None):
    width = both.shape[1]
    between = list(between)
    for t in range(n // (2 * spread)):
        s = base + 2 * spread * t
        x0, x1, x2, x3 = (h_ref[s + k * spread : s + (k + 1) * spread] for k in (-1, 0, 1, 2))
        rows = slice(t * spread, (t + 1) * spread)
        v[0, rows] = x0 - x2
        v[1, rows] = x1 + x2
        v[2, rows] = x2 - x1
        v[3, rows] = x1 - x3
    cols = dst.shape[1]
    for c in range(0, cols, 256):
        if between:
            between.pop(0)()
        q = slice(c, min(c + 256, cols))
        m1 = dot(v[0], conv_w[layer, 0:width, q])
        m4 = dot(v[3], conv_w[layer, 2 * width : 3 * width, q])
        if early is not None and c == 0:
            early()
        m2 = dot(v[1], both[0, :, q])
        m3 = dot(v[2], both[1, :, q])
        y0 = (m1 + (m2 + m3)).astype(BF)
        y1 = ((m2 - m3) - m4).astype(BF)
        for t in range(n // (2 * spread)):
            rows = slice(t * spread, (t + 1) * spread)
            at = 2 * spread * t
            dst[at : at + spread, q] = y0[rows]
            dst[at + spread : at + 2 * spread, q] = y1[rows]


def put_mid(z_ref, own, other, mid_ref, layer, start, n):
    for i, m in tiles(start, start + n, PIECE):
        scale = mid_ref[layer : layer + 1].astype(BF)
        z_ref[i : i + m] = gelu(
            (own[i : i + m] + other[i : i + m]) * scale
            + mid_ref[2 + layer : 3 + layer].astype(BF)
        )


def sigmoid(v):
    return 0.5 + 0.5 * jnp.tanh(0.5 * v)


def embed_edges(rows):
    def kernel(
        tower, dna, embed, ins, inb, mids, midb,
        e_a, e_b, codes, embed_v, s_in, b_in, own_mid, dna_v, ends, mids_v, midb_v, sem,
    ):
        cp = pltpu.make_async_copy
        step = 128
        copies = [
            cp(dna, dna_v, sem.at[0]), cp(embed, embed_v, sem.at[1]),
            cp(tower.at[pl.ds(0, HALO)], ends.at[0], sem.at[2]),
            cp(tower.at[pl.ds(rows - HALO, HALO)], ends.at[1], sem.at[3]),
            cp(ins, s_in, sem.at[4]), cp(inb, b_in, sem.at[5]),
            cp(mids, mids_v, sem.at[6]), cp(midb, midb_v, sem.at[7]),
        ]
        for c in copies:
            c.start()
        slots = dna.shape[0]
        row = lax.broadcasted_iota(jnp.int32, (4 * slots, slots), 0)
        col = lax.broadcasted_iota(jnp.int32, (4 * slots, slots), 1)
        spread_map = jnp.where((row >> 2) == col, 1.0, 0.0).astype(BF)
        code = (lax.broadcasted_iota(jnp.int32, (4 * slots, step), 0) & 3).astype(F32)
        for c in copies:
            c.wait()
        for i, n in tiles(0, rows, step):
            base = dot(spread_map, dna_v[:, i : i + n].astype(F32).astype(BF))
            codes[i : i + n] = jnp.where(base == code, 1.0, 0.0).T.astype(BF)
        even = lax.rem(lax.axis_index("seq"), 2) == 0
        low = (ends[0].astype(F32) + dot(codes[0:HALO], embed_v[...])).astype(BF)
        high = (ends[1].astype(F32) + dot(codes[rows - HALO : rows], embed_v[...])).astype(BF)
        e_a[...] = jnp.where(even, high, low)
        e_b[...] = jnp.where(even, low, high)
        first = lax.axis_index("chan") == 0
        mid = jnp.concatenate([mids_v[...], midb_v[...]], axis=0)
        own_mid[...] = jnp.concatenate(
            [jnp.where(first, mid, 0.0), jnp.where(first, 0.0, mid)], axis=1
        )

    return kernel


def embed_first(a_lo, a_hi, rows):
    def kernel(tower, codes, embed, s_in, b_in, conv_w, own_mid, x0, h0, pa, both, v):
        step = 128

        def embed_tile(i, n):
            x = tower[i : i + n].astype(F32) + dot(codes[i : i + n], embed[...])
            x0[i : i + n] = x.astype(BF)

        def act_tile(start, n):
            for i, m in tiles(start, start + n, PIECE):
                h0[i : i + m] = act_rows(x0[i : i + m], s_in, b_in, 0)

        work = tiles(0, rows, step)
        embed_tile(*work[0])

        def stage(t):
            if t + 1 < len(work):
                embed_tile(*work[t + 1])
            act_tile(*work[t])

        need = -(-(a_hi + D0) // step)
        for t in range(need):
            stage(t)
        later = [lambda t=t: stage(t) for t in range(need, len(work))]
        pair_conv(
            h0, a_lo, D0, a_hi - a_lo, conv_w, 0, both, pa, v, [lambda: None] + later[:2],
            lambda: put_weights(both, conv_w, 0, 0, both.shape[1]),
        )
        for f in later[2:]:
            f()
        mid = own_mid[...]
        big = mid.astype(BF)
        rest = mid - big.astype(F32)
        middle = rest.astype(BF)
        small = (rest - middle.astype(F32)).astype(BF)
        pa[a_hi - a_lo : a_hi - a_lo + EXTRA] = jnp.concatenate(
            [big.astype(F32), middle.astype(F32), small.astype(F32), jnp.zeros_like(mid)], axis=0
        ).astype(BF)

    return kernel


def first_rest(b_lo, b_hi):
    def kernel(h0, conv_w, both, pb, both_next, v):
        third = both.shape[1] // 3
        later = [
            lambda k=k: put_weights(both_next, conv_w, 1, k * third, (k + 1) * third)
            for k in range(3)
        ]
        pair_conv(h0, b_lo, D0, b_hi - b_lo, conv_w, 0, both, pb, v, later)

    return kernel


def first_edges(rows):
    def kernel(r_a, r_b, h0, conv_w, s_in, b_in, pe, lo, hi, ext):
        seq = lax.axis_index("seq")
        even = lax.rem(seq, 2) == 0
        inner = 2 * D0
        span = HALO + inner
        ext[HALO:span] = h0[0:inner]
        ext[span : span + inner] = h0[rows - inner : rows]
        ends = (
            (lo, r_b, r_a, 0, seq == 0),
            (hi, r_a, r_b, span + inner, seq == lax.axis_size("seq") - 1),
        )
        for i, m in tiles(0, HALO, PIECE):
            zero = jnp.zeros((m, h0.shape[1]), BF)
            for keep, at_even, at_odd, at, outside in ends:
                x = jnp.where(even, at_even[i : i + m], at_odd[i : i + m])
                keep[i : i + m] = x
                ext[at + i : at + i + m] = jnp.where(outside, zero, act_rows(x, s_in, b_in, 0))
        lhs = [taps(ext, s + D0, D0, HALO) for s in (0, span)]
        pe[...] = dot(jnp.concatenate(lhs, axis=0), conv_w[0]).astype(BF)

    return kernel


def second_first(a_lo, a_hi, c_lo, c_hi):
    def kernel(
        pa, ra, x0, point_w, conv_w, both, s_in, b_in, own_mid, x1a, h1a, qa, mid, z, acc, v,
    ):
        step = 128
        n_a = a_hi - a_lo
        tail = ra[n_a : n_a + EXTRA].astype(F32)
        mid[...] = own_mid[...] + (tail[0:4] + tail[4:8] + tail[8:12])
        work = tiles(0, n_a, step)

        def act_tile(start, n):
            for i, m in tiles(start, start + n, PIECE):
                x = (x0[a_lo + i : a_lo + i + m].astype(F32) + acc[i : i + m]).astype(BF)
                x1a[i : i + m] = x
                h1a[i : i + m] = act_rows(x, s_in, b_in, 1)

        put_mid(z, pa, ra, mid, 0, *work[0])
        for t in range(len(work) + 1):
            if t + 1 < len(work):
                put_mid(z, pa, ra, mid, 0, *work[t + 1])
            if 1 <= t <= len(work):
                act_tile(*work[t - 1])
            if t < len(work):
                i, n = work[t]
                acc[i : i + n] = dot(z[i : i + n], point_w[0])
        pair_conv(h1a, c_lo - a_lo, D1, c_hi - c_lo, conv_w, 1, both, qa, v)

    return kernel


def second_rest(rows, a_lo, a_hi, c_hi, e_hi):
    def kernel(
        pb, rb, x0, x1a, h1a, point_w, conv_w, both, mid, s_in, b_in, x1b, x1t, h1t, qb, h1, z, acc, v
    ):
        step = 224
        b_hi = rows - D0
        first = c_hi - D1
        h1[0 : a_hi - first] = h1a[first - a_lo : a_hi - a_lo]
        x1b[0 : a_hi - c_hi] = x1a[c_hi - a_lo : a_hi - a_lo]
        work = tiles(0, b_hi - a_hi, step)

        def act_tile(start, n):
            for i, m in tiles(start, start + n, PIECE):
                g = a_hi + i
                x = acc[i : i + m]
                h1[g - first : g - first + m] = act_rows(x, s_in, b_in, 1)
                keep = max(0, min(m, e_hi - g))
                if keep:
                    x1b[g - c_hi : g - c_hi + keep] = x[0:keep]
                if keep < m:
                    x1t[g + keep - e_hi : g + m - e_hi] = x[keep:]

        put_mid(z, pb, rb, mid, 0, *work[0])
        for t in range(len(work) + 1):
            if t + 1 < len(work):
                put_mid(z, pb, rb, mid, 0, *work[t + 1])
            if 1 <= t <= len(work):
                act_tile(*work[t - 1])
            if t < len(work):
                i, n = work[t]
                x = x0[a_hi + i : a_hi + i + n].astype(F32) + dot(z[i : i + n], point_w[0])
                acc[i : i + n] = x.astype(BF)
        pair_conv(h1, c_hi - first, D1, e_hi - c_hi, conv_w, 1, both, qb, v)
        h1t[...] = h1[e_hi - D1 - first : b_hi - first]

    return kernel


def second_edges(rows, a_lo, c_lo, e_hi):
    def kernel(
        pe, re, x0, lo, hi, x1a, h1a, x1t, h1t, point_w, conv_w, mid, s_in, b_in, x1c, qc, ext, z, acc
    ):
        seq = lax.axis_index("seq")
        tail = rows - D0 - e_hi
        top = c_lo + 2 * D1
        bottom = rows - e_hi + 2 * D1
        put_mid(z, pe, re, mid, 0, 0, 2 * HALO)
        acc[...] = dot(z[...], point_w[0])
        x1c[D0:c_lo] = x1a[0 : c_lo - a_lo]
        x1c[c_lo : c_lo + tail] = x1t[...]
        ext[HALO:top] = h1a[0 : c_lo + D1 - a_lo]
        ext[top : top + bottom - HALO] = h1t[...]
        low = top + bottom - HALO
        parts = (
            (0, 32, lo, HALO - D1, 0, None, seq == 0),
            (32, 16, lo, HALO - 16, 32, None, seq == 0),
            (D1, D0, x0, 0, D1, 0, None),
            (HALO, D0, x0, rows - D0, low, c_lo + tail, None),
            (HALO + D0, 32, hi, 0, low + D0, None, seq == lax.axis_size("seq") - 1),
            (HALO + D0 + 32, 16, hi, 32, low + D0 + 32, None, seq == lax.axis_size("seq") - 1),
        )
        for i, m, base, at, to, keep, outside in parts:
            x = (base[at : at + m].astype(F32) + acc[i : i + m]).astype(BF)
            h = act_rows(x, s_in, b_in, 1)
            if keep is not None:
                x1c[keep : keep + m] = x
            if outside is not None:
                h = jnp.where(outside, jnp.zeros_like(h), h)
            ext[to : to + m] = h
        lhs = [taps(ext, s + D1, D1, n) for s, n in ((0, c_lo), (top, rows - e_hi))]
        qc[...] = dot(jnp.concatenate(lhs, axis=0), conv_w[1]).astype(BF)

    return kernel


def own_half(width):
    chan = lax.axis_index("chan")
    mine = pl.ds(pl.multiple_of(chan * width, 128), width)
    theirs = pl.ds(pl.multiple_of((1 - chan) * width, 128), width)
    return mine, theirs


def last_point(x_base, n_rows, step, has_pool):
    def kernel(q, r, x1, point_w, mid, *rest):
        if has_pool:
            d_prev, pool, dm, xo, l_prev, z, acc, x2 = rest
        else:
            dm, xo, z, acc, x2 = rest
        half = step // 2
        row = lax.broadcasted_iota(jnp.int32, (step, step), 0)
        col = lax.broadcasted_iota(jnp.int32, (step, step), 1)
        pair = jnp.where(row < half, row, row - half) * 2
        pick = jnp.where(col == pair + 1, jnp.where(row < half, -1.0, 1.0), 0.0)
        pick = jnp.where((col == pair) & (row < half), 1.0, pick).astype(BF)

        def sum_rows(start, n):
            for i, m in tiles(start, start + n, PIECE):
                x = x1[x_base + i : x_base + i + m].astype(F32) + acc[i : i + m]
                x2[i : i + m] = x.astype(BF)

        def pair_rows(start, n):
            j = start // 2
            both = dot(pick, x2[start : start + n])
            dm[j : j + half] = both[:half].astype(BF)
            xo[j : j + half] = both[half:].astype(BF)

        work = tiles(0, n_rows, step)
        put_mid(z, q, r, mid, 1, *work[0])
        if has_pool:
            l_prev[...] = dot(d_prev[...], pool[own_half(x1.shape[1])[0], :])
        for t in range(len(work) + 2):
            if t + 1 < len(work):
                put_mid(z, q, r, mid, 1, *work[t + 1])
            if 1 <= t <= len(work):
                sum_rows(*work[t - 1])
            if t < len(work):
                i, n = work[t]
                acc[i : i + n] = dot(z[i : i + n], point_w[1])
            if t >= 2:
                pair_rows(*work[t - 2])

    return kernel


def finish(y, xo, d, logit):
    for i, m in tiles(0, y.shape[0], PIECE):
        y[i : i + m] = (
            xo[i : i + m].astype(F32) + sigmoid(logit[i : i + m]) * d[i : i + m].astype(F32)
        ).astype(BF)


def pool_first(ra, la, rb, dc, pool, da, xoa, db, xob, ya, yb, lc, acc_a, acc_b):
    mine, theirs = own_half(ra.shape[1])
    acc_a[...] = la[...] + dot(ra[...], pool[theirs, :])
    acc_b[...] = dot(db[...], pool[mine, :]) + dot(rb[...], pool[theirs, :])
    finish(ya, xoa, da, acc_a)
    lc[...] = dot(dc[...], pool[mine, :])
    finish(yb, xob, db, acc_b)


def pool_last(p_lo, p_hi, p_end):
    def kernel(rc, lc, pool, dc, xoc, ya, yb, out, y, acc, sem):
        theirs = own_half(rc.shape[1])[1]
        copy = pltpu.make_async_copy
        last = rc.shape[0] - p_lo
        copies = [
            copy(ya, out.at[pl.ds(p_lo, p_hi - p_lo)], sem.at[0]),
            copy(yb, out.at[pl.ds(p_hi, p_end - p_hi)], sem.at[1]),
            copy(y.at[pl.ds(0, p_lo)], out.at[pl.ds(0, p_lo)], sem.at[2]),
            copy(y.at[pl.ds(p_lo, last)], out.at[pl.ds(p_end, last)], sem.at[3]),
        ]
        copies[0].start()
        copies[1].start()
        acc[...] = lc[...] + dot(rc[...], pool[theirs, :])
        finish(y, xoc, dc, acc)
        copies[2].start()
        copies[3].start()
        for c in copies:
            c.wait()

    return kernel


def swap_chan(a):
    return lax.ppermute(a, "chan", [(0, 1), (1, 0)])


def local(
    tower_input, dna_bases, base_embed, in_scale, entry_norm_shift,
    conv_w, mid_scale, mid_shift, point_w, pooling_weight,
):
    rows, width = tower_input.shape
    inner = conv_w.shape[3]
    a_lo, a_hi = D0, rows // 2 + 32
    c_lo, c_hi, e_hi = 96, rows // 2 - 32, rows - 160
    b_hi = rows - D0
    n_a, n_b = a_hi - a_lo, b_hi - a_hi
    m_a, m_b = c_hi - c_lo, e_hi - c_hi
    m_c = rows - m_a - m_b
    dma = pltpu.SemaphoreType.DMA
    weights = conv_w.reshape(conv_w.shape[0], 3 * width, inner)
    e_a, e_b, codes, embed, s_in, b_in, own_mid = call(
        "k0",
        embed_edges(rows),
        [
            ((HALO, width), BF), ((HALO, width), BF), ((rows, base_embed.shape[0]), BF),
            (base_embed.shape, BF), ((2, width), F32), ((2, width), F32), ((4, inner), F32),
        ],
        [
            tower_input, dna_bases.T, base_embed, in_scale, entry_norm_shift, mid_scale, mid_shift,
        ],
        [],
        [
            pltpu.VMEM(dna_bases.shape[::-1], jnp.int32), pltpu.VMEM((2, HALO, width), BF),
            pltpu.VMEM(mid_scale.shape, F32), pltpu.VMEM(mid_shift.shape, F32), dma((8,)),
        ],
    )
    x0, h0, pa, both0 = call(
        "k1a",
        embed_first(a_lo, a_hi, rows),
        [
            ((rows, width), BF), ((rows, width), BF), ((n_a + EXTRA, inner), BF),
            ((2, width, inner), BF),
        ],
        [],
        [tower_input, codes, embed, s_in, b_in, weights, own_mid],
        [pltpu.VMEM((4, n_a // 2, width), BF)],
    )
    ra = swap_chan(pa)
    count = lax.axis_size("seq")
    pairs_a = [(i, i ^ 1) for i in range(count)]
    pairs_b = [(i, ((i - 1) ^ 1) + 1) for i in range(1, count - 1)]
    r_a = lax.ppermute(e_a, "seq", pairs_a)
    r_b = lax.ppermute(e_b, "seq", pairs_b)
    pb, both1 = call(
        "k1b",
        first_rest(a_hi, b_hi),
        [((n_b, inner), BF), ((2, width, inner), BF)],
        [],
        [h0, weights, both0],
        [pltpu.VMEM((4, n_b // 2, width), BF)],
    )
    rb = swap_chan(pb)
    x1a, h1a, qa, mid = call(
        "k2a",
        second_first(a_lo, a_hi, c_lo, c_hi),
        [
            ((n_a, width), BF), ((n_a, width), BF), ((m_a, inner), BF), ((4, inner), F32),
        ],
        [],
        [pa, ra, x0, point_w, weights, both1, s_in, b_in, own_mid],
        [
            pltpu.VMEM((n_a, inner), BF), pltpu.VMEM((n_a, width), F32),
            pltpu.VMEM((4, m_a // 2, width), BF),
        ],
    )
    sa = swap_chan(qa)
    pe, lo, hi = call(
        "k1e",
        first_edges(rows),
        [((2 * HALO, inner), BF), ((HALO, width), BF), ((HALO, width), BF)],
        [],
        [r_a, r_b, h0, weights, s_in, b_in],
        [pltpu.VMEM((2 * (HALO + 2 * D0), width), BF)],
    )
    re = swap_chan(pe)
    x1b, x1t, h1t, qb = call(
        "k2b",
        second_rest(rows, a_lo, a_hi, c_hi, e_hi),
        [
            ((m_b, width), BF), ((b_hi - e_hi, width), BF),
            ((b_hi - e_hi + D1, width), BF), ((m_b, inner), BF),
        ],
        [],
        [pb, rb, x0, x1a, h1a, point_w, weights, both1, mid, s_in, b_in],
        [
            pltpu.VMEM((b_hi - c_hi + D1, width), BF), pltpu.VMEM((n_b, inner), BF),
            pltpu.VMEM((n_b, width), BF), pltpu.VMEM((4, m_b // 2, width), BF),
        ],
    )
    sb = swap_chan(qb)
    x1c, qc = call(
        "k2c",
        second_edges(rows, a_lo, c_lo, e_hi),
        [((m_c, width), BF), ((m_c, inner), BF)],
        [],
        [pe, re, x0, lo, hi, x1a, h1a, x1t, h1t, point_w, weights, mid, s_in, b_in],
        [
            pltpu.VMEM((m_c + 4 * D1, width), BF), pltpu.VMEM((2 * HALO, inner), BF),
            pltpu.VMEM((2 * HALO, width), F32),
        ],
    )
    sc = swap_chan(qc)
    ends, halves = [], []
    for name, q, s, x1, base, m, step in (
        ("a", qa, sa, x1a, c_lo - a_lo, m_a, 128),
        ("b", qb, sb, x1b, 0, m_b, 128),
        ("c", qc, sc, x1c, 0, m_c, 128),
    ):
        before = [ends[0][0], pooling_weight] if name == "b" else []
        dm, xo, *half = call(
            "k3" + name,
            last_point(base, m, step, bool(before)),
            [((m // 2, width), BF), ((m // 2, width), BF)]
            + [((d.shape[0], width), F32) for d in before[:1]],
            [],
            [q, s, x1, point_w, mid, *before],
            [
                pltpu.VMEM((m, inner), BF), pltpu.VMEM((m, width), F32),
                pltpu.VMEM((m, width), BF),
            ],
        )
        halves += half
        ends.append((dm, swap_chan(dm), xo))
    (da, ta, xoa), (db, tb, xob), (dc, tc, xoc) = ends
    (la,) = halves
    ya, yb, lc = call(
        "k4",
        pool_first,
        [((m_a // 2, width), BF), ((m_b // 2, width), BF), ((m_c // 2, width), F32)],
        [],
        [ta, la, tb, dc, pooling_weight, da, xoa, db, xob],
        [pltpu.VMEM((m_a // 2, width), F32), pltpu.VMEM((m_b // 2, width), F32)],
    )
    vm = [
        pltpu.with_memory_space_constraint(a, pltpu.VMEM)
        for a in (tc, lc, pooling_weight, dc, xoc, ya, yb)
    ]
    return pl.pallas_call(
        pool_last(c_lo // 2, c_hi // 2, e_hi // 2),
        out_shape=jax.ShapeDtypeStruct((rows // 2, width), BF),
        in_specs=[VM] * 7,
        out_specs=HBM,
        scratch_shapes=[
            pltpu.VMEM((m_c // 2, width), BF), pltpu.VMEM((m_c // 2, width), F32), dma((4,)),
        ],
        compiler_params=pltpu.CompilerParams(vmem_limit_bytes=GRANT),
    )(*vm)


def solution(mesh):
    return jax.shard_map(
        local,
        mesh=mesh,
        in_specs=(
            P(("groups", "seq"), "chan"),
            P(("groups", "seq"), None),
            P(None, "chan"),
            P(None, "chan"),
            P(None, "chan"),
            P(None, None, "chan", None),
            P(None, "chan"),
            P(None, "chan"),
            P(None, None, "chan"),
            P(None, "chan"),
        ),
        out_specs=P(("groups", "seq"), "chan"),
        check_vma=False,
    )
```

```python
import jax
import jax.numpy as jnp
from jax import lax
from jax.experimental import pallas as pl
from jax.experimental.pallas import tpu as pltpu
from jax.sharding import PartitionSpec as P


D0 = 32
D1 = 48
HALO = D0 + D1
EXTRA = 16
PIECE = 32
COST = {"k0": 100}
BF = jnp.bfloat16
F32 = jnp.float32
VM = pl.BlockSpec(memory_space=pltpu.VMEM)
HBM = pl.BlockSpec(memory_space=pltpu.HBM)
GRANT = 14 << 20


def call(name, kernel, outs, hbm, vmem, scratch=(), grant=GRANT):
    hbm = [pltpu.with_memory_space_constraint(a, pltpu.HBM) for a in hbm]
    vmem = [pltpu.with_memory_space_constraint(a, pltpu.VMEM) for a in vmem]
    return pl.pallas_call(
        kernel,
        out_shape=[pltpu.VMEM(shape, dtype) for shape, dtype in outs],
        in_specs=[HBM] * len(hbm) + [VM] * len(vmem),
        out_specs=[VM] * len(outs),
        scratch_shapes=list(scratch),
        compiler_params=pltpu.CompilerParams(vmem_limit_bytes=grant),
        cost_estimate=pl.CostEstimate(
            flops=COST.get(name, 3) * 10**9, bytes_accessed=0, transcendentals=0
        ),
    )(*hbm, *vmem)


def gelu(v):
    inner = v * (BF(0.7978845608028654) + BF(0.035677408136300125) * (v * v))
    half = BF(0.5) * v
    return half + half * jnp.tanh(inner)


def dot(a, b):
    return jnp.dot(a, b, preferred_element_type=F32)


def tiles(start, stop, step):
    return [(i, min(step, stop - i)) for i in range(start, stop, step)]


def act_rows(x, s_ref, b_ref, layer):
    return gelu(x * s_ref[layer : layer + 1].astype(BF) + b_ref[layer : layer + 1].astype(BF))


def taps(h_ref, base, spread, n):
    return jnp.concatenate(
        [h_ref[base + k * spread : base + k * spread + n] for k in (-1, 0, 1)], axis=1
    )


def put_weights(dst, conv_w, layer, start, stop):
    width = dst.shape[1]
    half = BF(0.5)
    for i, m in tiles(start, stop, PIECE):
        outer = conv_w[layer, i : i + m] + conv_w[layer, 2 * width + i : 2 * width + i + m]
        outer = half * outer
        inner = half * conv_w[layer, width + i : width + i + m]
        dst[0, i : i + m] = outer + inner
        dst[1, i : i + m] = outer - inner


def pair_conv(h_ref, base, spread, n, conv_w, layer, both, dst, v, between=(), early=None):
    width = both.shape[1]
    between = list(between)
    for t in range(n // (2 * spread)):
        s = base + 2 * spread * t
        x0, x1, x2, x3 = (h_ref[s + k * spread : s + (k + 1) * spread] for k in (-1, 0, 1, 2))
        rows = slice(t * spread, (t + 1) * spread)
        v[0, rows] = x0 - x2
        v[1, rows] = x1 + x2
        v[2, rows] = x2 - x1
        v[3, rows] = x1 - x3
    cols = dst.shape[1]
    for c in range(0, cols, 256):
        if between:
            between.pop(0)()
        q = slice(c, min(c + 256, cols))
        m1 = dot(v[0], conv_w[layer, 0:width, q])
        m4 = dot(v[3], conv_w[layer, 2 * width : 3 * width, q])
        if early is not None and c == 0:
            early()
        m2 = dot(v[1], both[0, :, q])
        m3 = dot(v[2], both[1, :, q])
        y0 = (m1 + (m2 + m3)).astype(BF)
        y1 = ((m2 - m3) - m4).astype(BF)
        for t in range(n // (2 * spread)):
            rows = slice(t * spread, (t + 1) * spread)
            at = 2 * spread * t
            dst[at : at + spread, q] = y0[rows]
            dst[at + spread : at + 2 * spread, q] = y1[rows]


def put_mid(z_ref, own, other, mid_ref, layer, start, n):
    for i, m in tiles(start, start + n, PIECE):
        scale = mid_ref[layer : layer + 1].astype(BF)
        z_ref[i : i + m] = gelu(
            (own[i : i + m] + other[i : i + m]) * scale
            + mid_ref[2 + layer : 3 + layer].astype(BF)
        )


def sigmoid(v):
    return 0.5 + 0.5 * jnp.tanh(0.5 * v)


def embed_edges(rows):
    def kernel(
        tower, dna, embed, ins, inb, mids, midb,
        e_a, e_b, codes, embed_v, s_in, b_in, own_mid, dna_v, ends, mids_v, midb_v, sem,
    ):
        cp = pltpu.make_async_copy
        step = 128
        copies = [
            cp(dna, dna_v, sem.at[0]), cp(embed, embed_v, sem.at[1]),
            cp(tower.at[pl.ds(0, HALO)], ends.at[0], sem.at[2]),
            cp(tower.at[pl.ds(rows - HALO, HALO)], ends.at[1], sem.at[3]),
            cp(ins, s_in, sem.at[4]), cp(inb, b_in, sem.at[5]),
            cp(mids, mids_v, sem.at[6]), cp(midb, midb_v, sem.at[7]),
        ]
        for c in copies:
            c.start()
        slots = dna.shape[0]
        row = lax.broadcasted_iota(jnp.int32, (4 * slots, slots), 0)
        col = lax.broadcasted_iota(jnp.int32, (4 * slots, slots), 1)
        spread_map = jnp.where((row >> 2) == col, 1.0, 0.0).astype(BF)
        code = (lax.broadcasted_iota(jnp.int32, (4 * slots, step), 0) & 3).astype(F32)
        for c in copies:
            c.wait()
        for i, n in tiles(0, rows, step):
            base = dot(spread_map, dna_v[:, i : i + n].astype(F32).astype(BF))
            codes[i : i + n] = jnp.where(base == code, 1.0, 0.0).T.astype(BF)
        even = lax.rem(lax.axis_index("seq"), 2) == 0
        low = (ends[0].astype(F32) + dot(codes[0:HALO], embed_v[...])).astype(BF)
        high = (ends[1].astype(F32) + dot(codes[rows - HALO : rows], embed_v[...])).astype(BF)
        e_a[...] = jnp.where(even, high, low)
        e_b[...] = jnp.where(even, low, high)
        first = lax.axis_index("chan") == 0
        mid = jnp.concatenate([mids_v[...], midb_v[...]], axis=0)
        own_mid[...] = jnp.concatenate(
            [jnp.where(first, mid, 0.0), jnp.where(first, 0.0, mid)], axis=1
        )

    return kernel


def embed_first(a_lo, a_hi, rows):
    def kernel(tower, codes, embed, s_in, b_in, conv_w, own_mid, x0, h0, pa, both, v):
        step = 128

        def embed_tile(i, n):
            x = tower[i : i + n].astype(F32) + dot(codes[i : i + n], embed[...])
            x0[i : i + n] = x.astype(BF)

        def act_tile(start, n):
            for i, m in tiles(start, start + n, PIECE):
                h0[i : i + m] = act_rows(x0[i : i + m], s_in, b_in, 0)

        work = tiles(0, rows, step)
        embed_tile(*work[0])

        def stage(t):
            if t + 1 < len(work):
                embed_tile(*work[t + 1])
            act_tile(*work[t])

        need = -(-(a_hi + D0) // step)
        for t in range(need):
            stage(t)
        later = [lambda t=t: stage(t) for t in range(need, len(work))]
        pair_conv(
            h0, a_lo, D0, a_hi - a_lo, conv_w, 0, both, pa, v, [lambda: None] + later[:2],
            lambda: put_weights(both, conv_w, 0, 0, both.shape[1]),
        )
        for f in later[2:]:
            f()
        mid = own_mid[...]
        big = mid.astype(BF)
        rest = mid - big.astype(F32)
        middle = rest.astype(BF)
        small = (rest - middle.astype(F32)).astype(BF)
        pa[a_hi - a_lo : a_hi - a_lo + EXTRA] = jnp.concatenate(
            [big.astype(F32), middle.astype(F32), small.astype(F32), jnp.zeros_like(mid)], axis=0
        ).astype(BF)

    return kernel


def first_rest(b_lo, b_hi):
    def kernel(h0, conv_w, both, pb, both_next, v):
        third = both.shape[1] // 3
        later = [
            lambda k=k: put_weights(both_next, conv_w, 1, k * third, (k + 1) * third)
            for k in range(3)
        ]
        pair_conv(h0, b_lo, D0, b_hi - b_lo, conv_w, 0, both, pb, v, later)

    return kernel


def first_edges(rows):
    def kernel(r_a, r_b, h0, conv_w, s_in, b_in, pe, lo, hi, ext):
        seq = lax.axis_index("seq")
        even = lax.rem(seq, 2) == 0
        inner = 2 * D0
        span = HALO + inner
        ext[HALO:span] = h0[0:inner]
        ext[span : span + inner] = h0[rows - inner : rows]
        ends = (
            (lo, r_b, r_a, 0, seq == 0),
            (hi, r_a, r_b, span + inner, seq == lax.axis_size("seq") - 1),
        )
        for i, m in tiles(0, HALO, PIECE):
            zero = jnp.zeros((m, h0.shape[1]), BF)
            for keep, at_even, at_odd, at, outside in ends:
                x = jnp.where(even, at_even[i : i + m], at_odd[i : i + m])
                keep[i : i + m] = x
                ext[at + i : at + i + m] = jnp.where(outside, zero, act_rows(x, s_in, b_in, 0))
        lhs = [taps(ext, s + D0, D0, HALO) for s in (0, span)]
        pe[...] = dot(jnp.concatenate(lhs, axis=0), conv_w[0]).astype(BF)

    return kernel


def second_first(a_lo, a_hi, c_lo, c_hi):
    def kernel(
        pa, ra, x0, point_w, conv_w, both, s_in, b_in, own_mid, x1a, h1a, qa, mid, z, acc, v,
    ):
        step = 224
        n_a = a_hi - a_lo
        tail = ra[n_a : n_a + EXTRA].astype(F32)
        mid[...] = own_mid[...] + (tail[0:4] + tail[4:8] + tail[8:12])
        work = tiles(0, n_a, step)

        def act_tile(start, n):
            for i, m in tiles(start, start + n, PIECE):
                x = (x0[a_lo + i : a_lo + i + m].astype(F32) + acc[i : i + m]).astype(BF)
                x1a[i : i + m] = x
                h1a[i : i + m] = act_rows(x, s_in, b_in, 1)

        put_mid(z, pa, ra, mid, 0, *work[0])
        for t in range(len(work) + 1):
            if t + 1 < len(work):
                put_mid(z, pa, ra, mid, 0, *work[t + 1])
            if 1 <= t <= len(work):
                act_tile(*work[t - 1])
            if t < len(work):
                i, n = work[t]
                acc[i : i + n] = dot(z[i : i + n], point_w[0])
        pair_conv(h1a, c_lo - a_lo, D1, c_hi - c_lo, conv_w, 1, both, qa, v)

    return kernel


def second_rest(rows, a_lo, a_hi, c_hi, e_hi):
    def kernel(
        pb, rb, x0, x1a, h1a, point_w, conv_w, both, mid, s_in, b_in, x1b, x1t, h1t, qb, h1, z, acc, v
    ):
        step = 256
        b_hi = rows - D0
        first = c_hi - D1
        h1[0 : a_hi - first] = h1a[first - a_lo : a_hi - a_lo]
        x1b[0 : a_hi - c_hi] = x1a[c_hi - a_lo : a_hi - a_lo]
        work = tiles(0, b_hi - a_hi, step)

        def act_tile(start, n):
            for i, m in tiles(start, start + n, PIECE):
                g = a_hi + i
                x = acc[i : i + m]
                h1[g - first : g - first + m] = act_rows(x, s_in, b_in, 1)
                keep = max(0, min(m, e_hi - g))
                if keep:
                    x1b[g - c_hi : g - c_hi + keep] = x[0:keep]
                if keep < m:
                    x1t[g + keep - e_hi : g + m - e_hi] = x[keep:]

        put_mid(z, pb, rb, mid, 0, *work[0])
        for t in range(len(work) + 1):
            if t + 1 < len(work):
                put_mid(z, pb, rb, mid, 0, *work[t + 1])
            if 1 <= t <= len(work):
                act_tile(*work[t - 1])
            if t < len(work):
                i, n = work[t]
                x = x0[a_hi + i : a_hi + i + n].astype(F32) + dot(z[i : i + n], point_w[0])
                acc[i : i + n] = x.astype(BF)
        pair_conv(h1, c_hi - first, D1, e_hi - c_hi, conv_w, 1, both, qb, v)
        h1t[...] = h1[e_hi - D1 - first : b_hi - first]

    return kernel


def second_edges(rows, a_lo, c_lo, e_hi):
    def kernel(
        pe, re, x0, lo, hi, x1a, h1a, x1t, h1t, point_w, conv_w, mid, s_in, b_in, x1c, qc, ext, z, acc
    ):
        seq = lax.axis_index("seq")
        tail = rows - D0 - e_hi
        top = c_lo + 2 * D1
        bottom = rows - e_hi + 2 * D1
        put_mid(z, pe, re, mid, 0, 0, 2 * HALO)
        acc[...] = dot(z[...], point_w[0])
        x1c[D0:c_lo] = x1a[0 : c_lo - a_lo]
        x1c[c_lo : c_lo + tail] = x1t[...]
        ext[HALO:top] = h1a[0 : c_lo + D1 - a_lo]
        ext[top : top + bottom - HALO] = h1t[...]
        low = top + bottom - HALO
        parts = (
            (0, 32, lo, HALO - D1, 0, None, seq == 0),
            (32, 16, lo, HALO - 16, 32, None, seq == 0),
            (D1, D0, x0, 0, D1, 0, None),
            (HALO, D0, x0, rows - D0, low, c_lo + tail, None),
            (HALO + D0, 32, hi, 0, low + D0, None, seq == lax.axis_size("seq") - 1),
            (HALO + D0 + 32, 16, hi, 32, low + D0 + 32, None, seq == lax.axis_size("seq") - 1),
        )
        for i, m, base, at, to, keep, outside in parts:
            x = (base[at : at + m].astype(F32) + acc[i : i + m]).astype(BF)
            h = act_rows(x, s_in, b_in, 1)
            if keep is not None:
                x1c[keep : keep + m] = x
            if outside is not None:
                h = jnp.where(outside, jnp.zeros_like(h), h)
            ext[to : to + m] = h
        lhs = [taps(ext, s + D1, D1, n) for s, n in ((0, c_lo), (top, rows - e_hi))]
        qc[...] = dot(jnp.concatenate(lhs, axis=0), conv_w[1]).astype(BF)

    return kernel


def own_half(width):
    chan = lax.axis_index("chan")
    mine = pl.ds(pl.multiple_of(chan * width, 128), width)
    theirs = pl.ds(pl.multiple_of((1 - chan) * width, 128), width)
    return mine, theirs


def last_point(x_base, n_rows, step, has_pool):
    def kernel(q, r, x1, point_w, mid, *rest):
        if has_pool:
            d_prev, pool, dm, xo, l_prev, z, acc, x2 = rest
        else:
            dm, xo, z, acc, x2 = rest
        half = step // 2
        row = lax.broadcasted_iota(jnp.int32, (step, step), 0)
        col = lax.broadcasted_iota(jnp.int32, (step, step), 1)
        pair = jnp.where(row < half, row, row - half) * 2
        pick = jnp.where(col == pair + 1, jnp.where(row < half, -1.0, 1.0), 0.0)
        pick = jnp.where((col == pair) & (row < half), 1.0, pick).astype(BF)

        def sum_rows(start, n):
            for i, m in tiles(start, start + n, PIECE):
                x = x1[x_base + i : x_base + i + m].astype(F32) + acc[i : i + m]
                x2[i : i + m] = x.astype(BF)

        def pair_rows(start, n):
            j = start // 2
            both = dot(pick, x2[start : start + n])
            dm[j : j + half] = both[:half].astype(BF)
            xo[j : j + half] = both[half:].astype(BF)

        work = tiles(0, n_rows, step)
        put_mid(z, q, r, mid, 1, *work[0])
        if has_pool:
            l_prev[...] = dot(d_prev[...], pool[own_half(x1.shape[1])[0], :])
        for t in range(len(work) + 2):
            if t + 1 < len(work):
                put_mid(z, q, r, mid, 1, *work[t + 1])
            if 1 <= t <= len(work):
                sum_rows(*work[t - 1])
            if t < len(work):
                i, n = work[t]
                acc[i : i + n] = dot(z[i : i + n], point_w[1])
            if t >= 2:
                pair_rows(*work[t - 2])

    return kernel


def finish(y, xo, d, logit):
    for i, m in tiles(0, y.shape[0], PIECE):
        y[i : i + m] = (
            xo[i : i + m].astype(F32) + sigmoid(logit[i : i + m]) * d[i : i + m].astype(F32)
        ).astype(BF)


def pool_first(ra, la, rb, dc, pool, da, xoa, db, xob, ya, yb, lc, acc_a, acc_b):
    mine, theirs = own_half(ra.shape[1])
    acc_a[...] = la[...] + dot(ra[...], pool[theirs, :])
    acc_b[...] = dot(db[...], pool[mine, :]) + dot(rb[...], pool[theirs, :])
    finish(ya, xoa, da, acc_a)
    lc[...] = dot(dc[...], pool[mine, :])
    finish(yb, xob, db, acc_b)


def pool_last(p_lo, p_hi, p_end):
    def kernel(rc, lc, pool, dc, xoc, ya, yb, out, y, acc, sem):
        theirs = own_half(rc.shape[1])[1]
        copy = pltpu.make_async_copy
        last = rc.shape[0] - p_lo
        copies = [
            copy(ya, out.at[pl.ds(p_lo, p_hi - p_lo)], sem.at[0]),
            copy(yb, out.at[pl.ds(p_hi, p_end - p_hi)], sem.at[1]),
            copy(y.at[pl.ds(0, p_lo)], out.at[pl.ds(0, p_lo)], sem.at[2]),
            copy(y.at[pl.ds(p_lo, last)], out.at[pl.ds(p_end, last)], sem.at[3]),
        ]
        copies[0].start()
        copies[1].start()
        acc[...] = lc[...] + dot(rc[...], pool[theirs, :])
        finish(y, xoc, dc, acc)
        copies[2].start()
        copies[3].start()
        for c in copies:
            c.wait()

    return kernel


def swap_chan(a):
    return lax.ppermute(a, "chan", [(0, 1), (1, 0)])


def local(
    tower_input, dna_bases, base_embed, in_scale, entry_norm_shift,
    conv_w, mid_scale, mid_shift, point_w, pooling_weight,
):
    rows, width = tower_input.shape
    inner = conv_w.shape[3]
    a_lo, a_hi = D0, rows // 2 - 32
    c_lo, c_hi, e_hi = 96, rows // 2 - 128, rows - 160
    b_hi = rows - D0
    n_a, n_b = a_hi - a_lo, b_hi - a_hi
    m_a, m_b = c_hi - c_lo, e_hi - c_hi
    m_c = rows - m_a - m_b
    dma = pltpu.SemaphoreType.DMA
    weights = conv_w.reshape(conv_w.shape[0], 3 * width, inner)
    e_a, e_b, codes, embed, s_in, b_in, own_mid = call(
        "k0",
        embed_edges(rows),
        [
            ((HALO, width), BF), ((HALO, width), BF), ((rows, base_embed.shape[0]), BF),
            (base_embed.shape, BF), ((2, width), F32), ((2, width), F32), ((4, inner), F32),
        ],
        [
            tower_input, dna_bases.T, base_embed, in_scale, entry_norm_shift, mid_scale, mid_shift,
        ],
        [],
        [
            pltpu.VMEM(dna_bases.shape[::-1], jnp.int32), pltpu.VMEM((2, HALO, width), BF),
            pltpu.VMEM(mid_scale.shape, F32), pltpu.VMEM(mid_shift.shape, F32), dma((8,)),
        ],
    )
    x0, h0, pa, both0 = call(
        "k1a",
        embed_first(a_lo, a_hi, rows),
        [
            ((rows, width), BF), ((rows, width), BF), ((n_a + EXTRA, inner), BF),
            ((2, width, inner), BF),
        ],
        [],
        [tower_input, codes, embed, s_in, b_in, weights, own_mid],
        [pltpu.VMEM((4, n_a // 2, width), BF)],
    )
    ra = swap_chan(pa)
    count = lax.axis_size("seq")
    pairs_a = [(i, i ^ 1) for i in range(count)]
    pairs_b = [(i, ((i - 1) ^ 1) + 1) for i in range(1, count - 1)]
    r_a = lax.ppermute(e_a, "seq", pairs_a)
    r_b = lax.ppermute(e_b, "seq", pairs_b)
    pb, both1 = call(
        "k1b",
        first_rest(a_hi, b_hi),
        [((n_b, inner), BF), ((2, width, inner), BF)],
        [],
        [h0, weights, both0],
        [pltpu.VMEM((4, n_b // 2, width), BF)],
    )
    rb = swap_chan(pb)
    x1a, h1a, qa, mid = call(
        "k2a",
        second_first(a_lo, a_hi, c_lo, c_hi),
        [
            ((n_a, width), BF), ((n_a, width), BF), ((m_a, inner), BF), ((4, inner), F32),
        ],
        [],
        [pa, ra, x0, point_w, weights, both1, s_in, b_in, own_mid],
        [
            pltpu.VMEM((n_a, inner), BF), pltpu.VMEM((n_a, width), F32),
            pltpu.VMEM((4, m_a // 2, width), BF),
        ],
    )
    sa = swap_chan(qa)
    pe, lo, hi = call(
        "k1e",
        first_edges(rows),
        [((2 * HALO, inner), BF), ((HALO, width), BF), ((HALO, width), BF)],
        [],
        [r_a, r_b, h0, weights, s_in, b_in],
        [pltpu.VMEM((2 * (HALO + 2 * D0), width), BF)],
    )
    re = swap_chan(pe)
    x1b, x1t, h1t, qb = call(
        "k2b",
        second_rest(rows, a_lo, a_hi, c_hi, e_hi),
        [
            ((m_b, width), BF), ((b_hi - e_hi, width), BF),
            ((b_hi - e_hi + D1, width), BF), ((m_b, inner), BF),
        ],
        [],
        [pb, rb, x0, x1a, h1a, point_w, weights, both1, mid, s_in, b_in],
        [
            pltpu.VMEM((b_hi - c_hi + D1, width), BF), pltpu.VMEM((n_b, inner), BF),
            pltpu.VMEM((n_b, width), BF), pltpu.VMEM((4, m_b // 2, width), BF),
        ],
    )
    sb = swap_chan(qb)
    x1c, qc = call(
        "k2c",
        second_edges(rows, a_lo, c_lo, e_hi),
        [((m_c, width), BF), ((m_c, inner), BF)],
        [],
        [pe, re, x0, lo, hi, x1a, h1a, x1t, h1t, point_w, weights, mid, s_in, b_in],
        [
            pltpu.VMEM((m_c + 4 * D1, width), BF), pltpu.VMEM((2 * HALO, inner), BF),
            pltpu.VMEM((2 * HALO, width), F32),
        ],
    )
    sc = swap_chan(qc)
    ends, halves = [], []
    for name, q, s, x1, base, m, step in (
        ("a", qa, sa, x1a, c_lo - a_lo, m_a, 288),
        ("b", qb, sb, x1b, 0, m_b, 160),
        ("c", qc, sc, x1c, 0, m_c, 128),
    ):
        before = [ends[0][0], pooling_weight] if name == "b" else []
        dm, xo, *half = call(
            "k3" + name,
            last_point(base, m, step, bool(before)),
            [((m // 2, width), BF), ((m // 2, width), BF)]
            + [((d.shape[0], width), F32) for d in before[:1]],
            [],
            [q, s, x1, point_w, mid, *before],
            [
                pltpu.VMEM((m, inner), BF), pltpu.VMEM((m, width), F32),
                pltpu.VMEM((m, width), BF),
            ],
        )
        halves += half
        ends.append((dm, swap_chan(dm), xo))
    (da, ta, xoa), (db, tb, xob), (dc, tc, xoc) = ends
    (la,) = halves
    ya, yb, lc = call(
        "k4",
        pool_first,
        [((m_a // 2, width), BF), ((m_b // 2, width), BF), ((m_c // 2, width), F32)],
        [],
        [ta, la, tb, dc, pooling_weight, da, xoa, db, xob],
        [pltpu.VMEM((m_a // 2, width), F32), pltpu.VMEM((m_b // 2, width), F32)],
    )
    vm = [
        pltpu.with_memory_space_constraint(a, pltpu.VMEM)
        for a in (tc, lc, pooling_weight, dc, xoc, ya, yb)
    ]
    return pl.pallas_call(
        pool_last(c_lo // 2, c_hi // 2, e_hi // 2),
        out_shape=jax.ShapeDtypeStruct((rows // 2, width), BF),
        in_specs=[VM] * 7,
        out_specs=HBM,
        scratch_shapes=[
            pltpu.VMEM((m_c // 2, width), BF), pltpu.VMEM((m_c // 2, width), F32), dma((4,)),
        ],
        compiler_params=pltpu.CompilerParams(vmem_limit_bytes=GRANT),
    )(*vm)


def solution(mesh):
    return jax.shard_map(
        local,
        mesh=mesh,
        in_specs=(
            P(("groups", "seq"), "chan"),
            P(("groups", "seq"), None),
            P(None, "chan"),
            P(None, "chan"),
            P(None, "chan"),
            P(None, None, "chan", None),
            P(None, "chan"),
            P(None, "chan"),
            P(None, None, "chan"),
            P(None, "chan"),
        ),
        out_specs=P(("groups", "seq"), "chan"),
        check_vma=False,
    )
```
